32 devices in a mesh: row: 4 (over x, core), col: 8 (over z, y).
Axes of the slice: x: 2, y: 2, z: 4, core: 2. Of those that a mesh axis runs over, the one named last changes fastest.
Arguments:
- vectors: float32 [16, 4096], P(None, ('row', 'col')), may hold values from -12 to 12, as said below
- diag_energy: float32 [4096], P(('row', 'col')), may hold values from 0.5 to 4
- blocks: float32 [4, 192, 128, 128], P('row', 'col'), may hold values from -0.078125 to 0.078125
- block_row: int32 [4, 192], P('row', 'col'), may hold values from 0 to 7
- block_col: int32 [4, 192], P('row', 'col'), may hold values from 0 to 3
Outputs:
- image: float32 [16, 4096], P(None, ('row', 'col'))
- resid: float32 [16, 4096], P(None, ('row', 'col'))
The draws below stay inside these ranges and needn't reach their ends.
Inputs may be any that keep to these rules, and one draw needn't show every extreme that they name: `vectors`: each row of X holds independent entries; the Gram matrix X X^T is positive definite.
All inputs are finite; a program needn't handle non-finite values.
Results may differ from the reference program's by a relative error of at most 0.0003.
Values sent between devices are 32-bit elements; how exact they have to be, the bound alone decides.
A program may use at most 64 MiB of HBM per device.

```python
import math
import jax
import jax.numpy as jnp
from jax import lax

K = 16
BLK = 128
BPT = 24
SHARD = 128
NDIM = 4096
RB = 8
CB = 4
N_ROW = 4
N_COL = 8


def draw_vectors(key, part):
    first_key = jax.random.fold_in(jax.random.fold_in(key, 11), 0)
    position = jnp.arange(NDIM).astype(jnp.float32)
    scale = jnp.exp(math.log(3.0) * position / NDIM)
    values = jax.random.normal(first_key, (K, NDIM), jnp.float32) * scale[None, :]
    return jnp.clip(values, -12.0, 12.0).astype(jnp.float32)


def set_ends(array, own_key, low, largest):
    longest = array.shape.index(max(array.shape))
    spots = []
    for shift in (0, 1):
        where = [jax.random.randint(jax.random.fold_in(own_key, axis), (), 0, length) for axis, length in enumerate(array.shape)]
        where[longest] = (where[longest] + shift) % array.shape[longest]
        spots.append(tuple(where))
    return array.at[spots[0]].set(low).at[spots[1]].set(largest)


def level_of(rng, extent, cuts, smallest, top_value):
    factor_of, own = 1.0, jax.random.fold_in(rng, 6)
    for axis_at, parts in cuts:
        heights = jnp.exp(jax.random.uniform(jax.random.fold_in(own, axis_at), (parts,), jnp.float32, smallest / len(cuts), top_value / len(cuts)))
        factor_of = factor_of * jnp.repeat(heights, extent[axis_at] // parts).reshape([-1 if axis == axis_at else 1 for axis in range(len(extent))])
    return factor_of


def gaussian(key, dims, width, most, shards=(), dtype=jnp.bfloat16):
    level = level_of(key, dims, shards, -0.22, 0.18) if shards else 1.0
    result = jax.random.normal(key, dims, jnp.float32) * width * level
    return jnp.minimum(jnp.maximum(result, -most), most).astype(dtype)


def setup_inputs(seed: int = 0) -> dict:
    splits = jax.random.split(jax.random.key(seed), 6)
    vectors = draw_vectors(jax.random.fold_in(splits[5], 71), 0)
    diag_energy = jnp.clip(jnp.exp(math.log(4.0) - 2.0794415 * jax.random.uniform(splits[1], (NDIM,), jnp.float32) ** level_of(splits[1], (NDIM,), ((0, 32),), -0.2, 0.2)), 0.5, 4.0)
    blocks = gaussian(splits[2], (N_ROW, N_COL * BPT, BLK, BLK), (2 * BPT * BLK * BLK // SHARD) ** -0.5, 0.078125, ((0, 4), (1, 8)), jnp.float32)
    block_row = set_ends(jax.random.randint(splits[3], (N_ROW, N_COL * BPT), 0, RB), jax.random.fold_in(splits[3], 1), 0, RB - 1).astype(jnp.int32)
    block_col = set_ends(jax.random.randint(splits[4], (N_ROW, N_COL * BPT), 0, CB), jax.random.fold_in(splits[4], 1), 0, CB - 1).astype(jnp.int32)
    return {"vectors": vectors, "diag_energy": diag_energy, "blocks": blocks, "block_row": block_row, "block_col": block_col}


def solve_metric(metric, gram):
    highest = lax.Precision.HIGHEST
    order = metric.shape[0]
    index = jnp.arange(order).astype(jnp.int32)
    factor = jnp.zeros_like(metric)
    for column in range(order):
        onehot = (index == column).astype(jnp.float32)
        rest = metric[:, column] - jnp.dot(factor, factor[column, :], precision=highest)
        pivot = jnp.sqrt(rest[column])
        values = jnp.where(index >= column, rest / pivot, 0.0)
        factor = factor + values[:, None] * onehot[None, :]
    inner = jnp.zeros_like(gram)
    for line in range(order):
        onehot = (index == line).astype(jnp.float32)
        value = (gram[line, :] - jnp.dot(factor[line, :], inner, precision=highest)) / factor[line, line]
        inner = inner + onehot[:, None] * value[None, :]
    solved = jnp.zeros_like(gram)
    for line in range(order - 1, -1, -1):
        onehot = (index == line).astype(jnp.float32)
        value = (inner[line, :] - jnp.dot(factor[:, line], solved, precision=highest)) / factor[line, line]
        solved = solved + onehot[:, None] * value[None, :]
    return solved

def reference(vectors, diag_energy, blocks, block_row, block_col):
    highest = lax.Precision.HIGHEST
    row_blocks = SHARD * N_COL // BLK
    col_blocks = SHARD * N_ROW // BLK
    xvec = vectors
    xrow = xvec.reshape(K, N_ROW, row_blocks, BLK).transpose(1, 0, 2, 3)
    xcol = xvec.reshape(K, N_ROW, N_COL, SHARD).transpose(0, 2, 1, 3).reshape(K, N_COL, col_blocks, BLK)
    tile_col = (jnp.arange(N_COL * BPT) // BPT).astype(jnp.int32)
    row_iota = jnp.arange(row_blocks).astype(jnp.int32)
    col_iota = jnp.arange(N_COL * col_blocks).astype(jnp.int32)

    def one_row(carry, inputs):
        tiles, rows_here, cols_here, xr_here = inputs
        picked = xcol[:, tile_col, cols_here]
        terms = jnp.einsum('bij,kbj->kbi', tiles, picked, precision=highest)
        onehot = (rows_here[:, None] == row_iota[None, :]).astype(jnp.float32)
        part_one = jnp.einsum('kbi,br->kri', terms, onehot, precision=highest)
        picked_two = xr_here[:, rows_here]
        terms_two = jnp.einsum('bij,kbi->kbj', tiles, picked_two, precision=highest)
        onehot_two = ((tile_col * col_blocks + cols_here)[:, None] == col_iota[None, :]).astype(jnp.float32)
        part_two = jnp.einsum('kbj,bq->kqj', terms_two, onehot_two, precision=highest)
        return (carry + part_two, part_one)
    start = jnp.zeros((K, N_COL * col_blocks, BLK), jnp.float32)
    col_sum, row_parts = lax.scan(one_row, start, (blocks, block_row, block_col, xrow))
    first = row_parts.transpose(1, 0, 2, 3).reshape(K, NDIM)
    second = col_sum.reshape(K, N_COL, N_ROW, SHARD).transpose(0, 2, 1, 3).reshape(K, NDIM)
    image = first + second + diag_energy[None, :] * xvec
    gram = jnp.dot(xvec, image.T, precision=highest, preferred_element_type=jnp.float32)
    metric = jnp.dot(xvec, xvec.T, precision=highest, preferred_element_type=jnp.float32)
    coef = solve_metric(metric, gram)
    resid = image - jnp.dot(coef.T, xvec, precision=highest, preferred_element_type=jnp.float32)
    return (image, resid)
```

```python
import functools

import jax
import jax.numpy as jnp
from jax import lax
from jax.experimental import pallas as pl
from jax.experimental.pallas import tpu as pltpu
from jax.sharding import PartitionSpec as P

BLK = 128
DIRECT = 64
F32 = jnp.float32
BF16 = jnp.bfloat16
MESH = pl.DeviceIdType.MESH


def halves(x):
    high = x.astype(BF16)
    return high, (x - high.astype(F32)).astype(BF16)


def add(terms):
    while len(terms) > 1:
        terms = [a + b for a, b in zip(terms[::2], terms[1::2])] + terms[len(terms) & ~1:]
    return terms[0]


def dot_nt(a, b):
    return lax.dot_general(a, b, (((1,), (1,)), ((), ())), preferred_element_type=F32)


def dot_nn(a, b):
    return lax.dot_general(a, b, (((1,), (0,)), ((), ())), preferred_element_type=F32)


def drain(ref, sem):
    pltpu.make_async_copy(ref, ref, sem).wait()


def kernel(
    n_row, n_col,
    x_hbm, diag_hbm, rows_hbm, cols_hbm, blocks_hbm,
    out_ref,
    x_ref, diag_ref, rows_ref, cols_ref, tiles, split, col_x, row_x, col_lhs, row_lhs,
    met_in, p1_out, p1_in, p2_out, p2_in, g1_out, g1_in, g2_out, g2_in, sent,
    load_sem, send, cx_r, rx_r, m_r, p1_r, p2_r, g1_r, g2_r,
):
    count = x_ref.shape[0]
    n_blk = tiles.shape[0]
    my_row = lax.axis_index("row")
    my_col = lax.axis_index("col")
    direct = n_row * n_col <= DIRECT

    def push(source, target, recv, peer):
        pltpu.make_async_remote_copy(
            src_ref=source, dst_ref=target, send_sem=send, recv_sem=recv,
            device_id=peer, device_id_type=MESH,
        ).start()

    def others(size, me):
        return [lax.rem(me + d, size) for d in range(1, size)]

    barrier = pltpu.get_barrier_semaphore()
    for peer in others(n_col, my_col):
        pl.semaphore_signal(barrier, inc=1, device_id={"col": peer}, device_id_type=MESH)
    for peer in others(n_row, my_row):
        pl.semaphore_signal(barrier, inc=1, device_id={"row": peer}, device_id_type=MESH)

    x_load, *small_loads, load = [
        pltpu.make_async_copy(source, target, load_sem.at[at])
        for at, (source, target) in enumerate(
            [(x_hbm, x_ref), (diag_hbm, diag_ref), (rows_hbm, rows_ref), (cols_hbm, cols_ref),
             (blocks_hbm.at[0], tiles)]
        )
    ]
    for copy in [x_load, *small_loads, load]:
        copy.start()
    x_load.wait()
    pl.semaphore_wait(barrier, n_row + n_col - 2)

    upper = my_col // (n_col // 2)
    for at in range(1, n_col):
        far = upper * at + (1 - upper) * (n_col - at)
        push(x_ref, row_x.at[my_col], rx_r, {"col": lax.rem(my_col + far, n_col)})
    for peer in others(n_row, my_row):
        push(x_ref, col_x.at[my_row], cx_r, {"row": peer})
    x_own = x_ref[...]
    row_x[my_col] = x_own
    col_x[my_row] = x_own

    for copy in [*small_loads, load]:
        copy.wait()
    for b in range(n_blk):
        high, low = halves(tiles[b])
        split[b] = jnp.concatenate([high, low], axis=1)

    per = BLK // count
    groups = count // 8
    lane = lax.broadcasted_iota(jnp.int32, (count, BLK), 1)
    sub = lax.broadcasted_iota(jnp.int32, (count, BLK), 0)
    keep = (lane // count) == (sub % per)

    def fold(o):
        return o[:count, :count] + o[count:, :count] + o[:count, count:]

    def pack(square):
        spread = jnp.where(keep, jnp.concatenate([square] * per, axis=1), 0.0)
        return jnp.concatenate(
            [jnp.sum(spread[g * per:(g + 1) * per], axis=0, keepdims=True) for g in range(groups)], axis=0
        )

    def unpack(packed):
        wide = jnp.concatenate(
            [jnp.broadcast_to(packed[g:g + 1], (per, BLK)) for g in range(groups)], axis=0
        )
        return jnp.where(keep, wide, 0.0)

    drain(col_x.at[pl.ds(0, n_row - 1)], cx_r)
    zero = jnp.zeros((count, BLK), BF16)
    col_two = []
    for q in range(n_row):
        high, low = halves(col_x[q])
        col_lhs[q] = jnp.concatenate(
            [jnp.concatenate([high, high], axis=1), jnp.concatenate([low, zero], axis=1)], axis=0
        )
        col_two.append(jnp.concatenate([high, low], axis=0))
    x_wide = jnp.concatenate(col_two, axis=1)
    met_in[my_col] = pack(fold(dot_nt(x_wide, x_wide)))
    for peer in others(n_col, my_col):
        push(met_in.at[my_col], met_in.at[my_col], m_r, {"col": peer})

    part_one = [jnp.zeros((count, BLK), F32) for _ in range(n_col)]
    for b in range(n_blk):
        o = dot_nt(col_lhs[cols_ref[0, b]], split[b])
        term = o[:count] + o[count:]
        place = rows_ref[0, b]
        for r in range(n_col):
            part_one[r] = part_one[r] + (place == r).astype(F32) * term
    for r in range(n_col):
        p1_out[r] = part_one[r]
    for d, peer in enumerate(others(n_col, my_col)):
        push(p1_out.at[peer], p1_in.at[d], p1_r, {"col": peer})

    own_diag = diag_ref[...] * x_own
    left = [jnp.concatenate(halves(x_own), axis=0)]
    right = [jnp.concatenate(halves(own_diag), axis=0)]
    p_two = [jnp.concatenate(halves(part), axis=0) for part in part_one]

    drain(row_x.at[pl.ds(0, n_col - 1)], rx_r)
    for at in range(n_col):
        both = jnp.concatenate(halves(row_x[at]), axis=0)
        row_lhs[at] = both
        left += [both, p_two[at]]
        right += [p_two[at], both]
    packed = pack(fold(dot_nt(jnp.concatenate(left, axis=1), jnp.concatenate(right, axis=1))))
    if direct:
        me = my_col * n_row + my_row
        g1_in[me] = packed
        for at in range(n_row * n_col - 1):
            to = at + (at >= me).astype(jnp.int32)
            push(
                g1_in.at[me], g1_in.at[me], g1_r,
                {"row": lax.rem(to, n_row), "col": to // n_row},
            )
    else:
        g1_out[...] = packed
        for d, peer in enumerate(others(n_row, my_row)):
            push(g1_out, g1_in.at[d], g1_r, {"row": peer})

    part_two = [jnp.zeros((count, BLK), F32) for _ in range(n_row)]
    for b in range(n_blk):
        o = dot_nn(row_lhs[rows_ref[0, b]], split[b])
        term = o[:count, :BLK] + o[count:, :BLK] + o[:count, BLK:]
        place = cols_ref[0, b]
        for q in range(n_row):
            part_two[q] = part_two[q] + (place == q).astype(F32) * term
    for q in range(n_row):
        p2_out[q] = part_two[q]
    for d, peer in enumerate(others(n_row, my_row)):
        push(p2_out.at[peer], p2_in.at[d], p2_r, {"row": peer})

    if not direct:
        drain(g1_in.at[pl.ds(0, n_row - 1)], g1_r)
        g2_out[...] = add([g1_out[...]] + [g1_in[d] for d in range(n_row - 1)])
        for d, peer in enumerate(others(n_col, my_col)):
            push(g2_out, g2_in.at[d], g2_r, {"col": peer})

    drain(met_in.at[pl.ds(0, n_col - 1)], m_r)
    metric = unpack(add([met_in[d] for d in range(n_col)]))
    shift = count
    while shift < BLK:
        metric = metric + pltpu.roll(metric, shift, 1)
        shift *= 2
    lines = [jnp.broadcast_to(metric[:, k:k + 1], (count, BLK)) for k in range(count)]
    solved = x_own
    pivots = jnp.ones((count, BLK), F32)
    for k in range(count):
        pivot = lines[k][k:k + 1]
        pivots = jnp.where(sub == k, pivot, pivots)
        ratio = jnp.where(sub == k, 0.0, lines[k] / pivot)
        solved = solved - ratio * solved[k:k + 1]
        for j in range(k + 1, count):
            lines[j] = lines[j] - ratio * lines[j][k:k + 1]
    high, low = halves(solved / pivots)
    y_two = jnp.concatenate(
        [jnp.concatenate([high] * per, axis=0), jnp.concatenate([low] * per, axis=0)], axis=1
    )

    drain(p2_in.at[pl.ds(0, n_row - 1)], p2_r)
    image = own_diag + p2_out[my_row]
    for d in range(n_row - 1):
        image = image + p2_in[d]
    drain(p1_in.at[pl.ds(0, n_col - 1)], p1_r)
    image = add([image, p1_out[my_col]] + [p1_in[d] for d in range(n_col - 1)])
    out_ref[0] = image

    if direct:
        drain(g1_in.at[pl.ds(0, n_row * n_col - 1)], g1_r)
        gram = add([g1_in[d] for d in range(n_row * n_col)])
    else:
        drain(g2_in.at[pl.ds(0, n_col - 1)], g2_r)
        gram = add([g2_out[...]] + [g2_in[d] for d in range(n_col - 1)])
    wide = unpack(gram)
    o = dot_nn(jnp.concatenate(halves(wide), axis=0), y_two)
    out_ref[1] = image - (o[:count, :BLK] + o[count:, :BLK] + o[:count, BLK:])
    drain(sent, send)


def part_kernel(both_ref, image_ref, resid_ref):
    image_ref[...] = both_ref[0]
    resid_ref[...] = both_ref[1]


def per_device(n_row, n_col, vectors, diag_energy, blocks, block_row, block_col):
    count = vectors.shape[0]
    n_blk = blocks.shape[1]
    groups = count // 8
    piece = (count, BLK)
    direct = n_row * n_col <= DIRECT
    n_all = n_row * n_col if direct else n_row
    pieces = 2 * (n_row + n_col - 2)
    small = n_col - 1 + n_all - 1 + (0 if direct else n_col - 1)
    vmem = pl.BlockSpec(memory_space=pltpu.VMEM)
    dma = pltpu.SemaphoreType.DMA
    both = pl.pallas_call(
        functools.partial(kernel, n_row, n_col),
        out_shape=pltpu.VMEM((2,) + piece, F32),
        in_specs=[pl.BlockSpec(memory_space=pl.ANY)] * 5,
        out_specs=vmem,
        scratch_shapes=[
            pltpu.VMEM(piece, F32),
            pltpu.VMEM((1, BLK), F32),
            pltpu.SMEM((1, n_blk), jnp.int32),
            pltpu.SMEM((1, n_blk), jnp.int32),
            pltpu.VMEM((n_blk, BLK, BLK), F32),
            pltpu.VMEM((n_blk, BLK, 2 * BLK), BF16),
            pltpu.VMEM((n_row,) + piece, F32),
            pltpu.VMEM((n_col,) + piece, F32),
            pltpu.VMEM((n_row, 2 * count, 2 * BLK), BF16),
            pltpu.VMEM((n_col, 2 * count, BLK), BF16),
            pltpu.VMEM((n_col, groups, BLK), F32),
            pltpu.VMEM((n_col,) + piece, F32),
            pltpu.VMEM((n_col - 1,) + piece, F32),
            pltpu.VMEM((n_row,) + piece, F32),
            pltpu.VMEM((n_row - 1,) + piece, F32),
            pltpu.VMEM((groups, BLK), F32),
            pltpu.VMEM((n_all, groups, BLK), F32),
            pltpu.VMEM((groups, BLK), F32),
            pltpu.VMEM((n_col, groups, BLK), F32),
            pltpu.VMEM((8 * pieces + small, groups, BLK), F32),
            dma((5,)),
            dma, dma, dma, dma, dma, dma, dma, dma,
        ],
        compiler_params=pltpu.CompilerParams(collective_id=0, has_side_effects=True),
    )(vectors, diag_energy.reshape(1, -1), block_row, block_col, blocks)
    return pl.pallas_call(
        part_kernel,
        out_shape=[jax.ShapeDtypeStruct(piece, F32)] * 2,
        in_specs=[vmem],
        out_specs=[vmem, vmem],
    )(pltpu.with_memory_space_constraint(both, pltpu.VMEM))


def solution(mesh):
    return jax.shard_map(
        functools.partial(per_device, mesh.shape["row"], mesh.shape["col"]),
        mesh=mesh,
        in_specs=(
            P(None, ("row", "col")),
            P(("row", "col")),
            P("row", "col", None, None),
            P("row", "col"),
            P("row", "col"),
        ),
        out_specs=(P(None, ("row", "col")), P(None, ("row", "col"))),
        check_vma=False,
    )
```

```python
import functools

import jax
import jax.numpy as jnp
from jax import lax
from jax.experimental import pallas as pl
from jax.experimental.pallas import tpu as pltpu
from jax.sharding import PartitionSpec as P

BLK = 128
DIRECT = 64
FAST = 2
F32 = jnp.float32
BF16 = jnp.bfloat16
MESH = pl.DeviceIdType.MESH


def halves(x):
    high = x.astype(BF16)
    return high, (x - high.astype(F32)).astype(BF16)


def add(terms):
    while len(terms) > 1:
        terms = [a + b for a, b in zip(terms[::2], terms[1::2])] + terms[len(terms) & ~1:]
    return terms[0]


def dot_nt(a, b):
    return lax.dot_general(a, b, (((1,), (1,)), ((), ())), preferred_element_type=F32)


def dot_nn(a, b):
    return lax.dot_general(a, b, (((1,), (0,)), ((), ())), preferred_element_type=F32)


def drain(ref, sem):
    pltpu.make_async_copy(ref, ref, sem).wait()


def kernel(
    n_row, n_col,
    x_hbm, diag_hbm, rows_hbm, cols_hbm, blocks_hbm,
    out_ref,
    x_ref, diag_ref, rows_ref, cols_ref, tiles, split, col_x, row_x, col_lhs, row_lhs,
    met_in, p1_out, p1_in, p2_out, p2_in, g1_out, g1_in, g2_out, g2_in, sent, far_p1, far_g, far_sum,
    load_sem, send, cx_r, rx_r, m_r, p1_r, p2_r, g1_r, g2_r, far_s, far_r,
):
    count = x_ref.shape[0]
    n_blk = tiles.shape[0]
    my_row = lax.axis_index("row")
    my_col = lax.axis_index("col")
    direct = n_row * n_col <= DIRECT

    last = my_col == n_col - 1
    first = (my_col == 0) & (my_row < FAST)

    def push(source, target, recv, peer, sem=send):
        pltpu.make_async_remote_copy(
            src_ref=source, dst_ref=target, send_sem=sem, recv_sem=recv,
            device_id=peer, device_id_type=MESH,
        ).start()

    def others(size, me):
        return [lax.rem(me + d, size) for d in range(1, size)]

    barrier = pltpu.get_barrier_semaphore()
    for peer in others(n_col, my_col):
        pl.semaphore_signal(barrier, inc=1, device_id={"col": peer}, device_id_type=MESH)
    for peer in others(n_row, my_row):
        pl.semaphore_signal(barrier, inc=1, device_id={"row": peer}, device_id_type=MESH)

    x_load, *small_loads, load = [
        pltpu.make_async_copy(source, target, load_sem.at[at])
        for at, (source, target) in enumerate(
            [(x_hbm, x_ref), (diag_hbm, diag_ref), (rows_hbm, rows_ref), (cols_hbm, cols_ref),
             (blocks_hbm.at[0], tiles)]
        )
    ]
    for copy in [x_load, *small_loads, load]:
        copy.start()
    x_load.wait()
    pl.semaphore_wait(barrier, n_row + n_col - 2)

    mirror = n_col - 1 - my_col
    upper = my_col // (n_col // 2)
    for at in range(1, n_col):
        far = upper * at + (1 - upper) * (n_col - at)
        peer = lax.rem(my_col + far, n_col)
        push(x_ref, row_x.at[my_col], rx_r.at[(peer == mirror).astype(jnp.int32)], {"col": peer})
    for peer in others(n_row, my_row):
        push(x_ref, col_x.at[my_row], cx_r, {"row": peer})
    x_own = x_ref[...]
    row_x[my_col] = x_own
    col_x[my_row] = x_own

    for copy in [*small_loads, load]:
        copy.wait()
    for b in range(n_blk):
        high, low = halves(tiles[b])
        split[b] = jnp.concatenate([high, low], axis=1)

    per = BLK // count
    groups = count // 8
    lane = lax.broadcasted_iota(jnp.int32, (count, BLK), 1)
    sub = lax.broadcasted_iota(jnp.int32, (count, BLK), 0)
    keep = (lane // count) == (sub % per)

    def fold(o):
        return o[:count, :count] + o[count:, :count] + o[:count, count:]

    def pack(square):
        spread = jnp.where(keep, jnp.concatenate([square] * per, axis=1), 0.0)
        return jnp.concatenate(
            [jnp.sum(spread[g * per:(g + 1) * per], axis=0, keepdims=True) for g in range(groups)], axis=0
        )

    def unpack(packed):
        wide = jnp.concatenate(
            [jnp.broadcast_to(packed[g:g + 1], (per, BLK)) for g in range(groups)], axis=0
        )
        return jnp.where(keep, wide, 0.0)

    drain(col_x.at[pl.ds(0, n_row - 1)], cx_r)
    zero = jnp.zeros((count, BLK), BF16)
    col_two = []
    for q in range(n_row):
        high, low = halves(col_x[q])
        col_lhs[q] = jnp.concatenate(
            [jnp.concatenate([high, high], axis=1), jnp.concatenate([low, zero], axis=1)], axis=0
        )
        col_two.append(jnp.concatenate([high, low], axis=0))
    x_wide = jnp.concatenate(col_two, axis=1)
    met_in[my_col] = pack(fold(dot_nt(x_wide, x_wide)))
    for peer in others(n_col, my_col):
        push(met_in.at[my_col], met_in.at[my_col], m_r, {"col": peer})

    part_one = [jnp.zeros((count, BLK), F32) for _ in range(n_col)]
    for b in range(n_blk):
        o = dot_nt(col_lhs[cols_ref[0, b]], split[b])
        term = o[:count] + o[count:]
        place = rows_ref[0, b]
        for r in range(n_col):
            part_one[r] = part_one[r] + (place == r).astype(F32) * term
    for r in range(n_col):
        p1_out[r] = part_one[r]
    if direct:
        @pl.when(last)
        def _():
            for row in range(FAST):
                push(p1_out.at[0], far_p1.at[my_row], far_r, {"row": row, "col": 0}, far_s)
    for d, peer in enumerate(others(n_col, my_col)):
        push(p1_out.at[peer], p1_in.at[d], p1_r, {"col": peer})

    own_diag = diag_ref[...] * x_own
    left = [jnp.concatenate(halves(x_own), axis=0)]
    right = [jnp.concatenate(halves(own_diag), axis=0)]
    order = [lax.rem(mirror + k, n_col) for k in range(1, n_col)] + [mirror]
    p_two = [jnp.concatenate(halves(p1_out[at]), axis=0) for at in order]

    def products(left, right):
        return pack(fold(dot_nt(jnp.concatenate(left, axis=1), jnp.concatenate(right, axis=1))))

    def take(at, p_at):
        both = jnp.concatenate(halves(row_x[at]), axis=0)
        row_lhs[at] = both
        return [both, p_at], [p_at, both]

    def spread_out(ats, me):
        for at in ats:
            to = at + (at >= me).astype(jnp.int32)
            push(
                g1_in.at[me], g1_in.at[me], g1_r,
                {"row": lax.rem(to, n_row), "col": to // n_row},
            )

    me = my_col * n_row + my_row
    drain(row_x.at[pl.ds(0, n_col - 2)], rx_r.at[0])
    for at, p_at in zip(order[:-1], p_two):
        one, two = take(at, p_at)
        left += one
        right += two
    packed = products(left, right)
    if direct:
        far_g[...] = packed

        @pl.when(last)
        def _():
            for row in range(FAST):
                push(far_g, g1_in.at[me], g1_r, {"row": row, "col": 0})

    drain(row_x.at[pl.ds(0, 1)], rx_r.at[1])
    packed = packed + products(*take(mirror, p_two[-1]))
    if direct:
        g1_in[me] = packed

        @pl.when(jnp.logical_not(last))
        def _():
            spread_out(range(FAST), me)

        spread_out(range(FAST, n_row * n_col - 1), me)
    else:
        g1_out[...] = packed
        for d, peer in enumerate(others(n_row, my_row)):
            push(g1_out, g1_in.at[d], g1_r, {"row": peer})

    part_two = [jnp.zeros((count, BLK), F32) for _ in range(n_row)]
    for b in range(n_blk):
        o = dot_nn(row_lhs[rows_ref[0, b]], split[b])
        term = o[:count, :BLK] + o[count:, :BLK] + o[:count, BLK:]
        place = cols_ref[0, b]
        for q in range(n_row):
            part_two[q] = part_two[q] + (place == q).astype(F32) * term
    for q in range(n_row):
        p2_out[q] = part_two[q]
    for d, peer in enumerate(others(n_row, my_row)):
        push(p2_out.at[peer], p2_in.at[d], p2_r, {"row": peer})

    if not direct:
        drain(g1_in.at[pl.ds(0, n_row - 1)], g1_r)
        g2_out[...] = add([g1_out[...]] + [g1_in[d] for d in range(n_row - 1)])
        for d, peer in enumerate(others(n_col, my_col)):
            push(g2_out, g2_in.at[d], g2_r, {"col": peer})

    drain(met_in.at[pl.ds(0, n_col - 1)], m_r)
    metric = unpack(add([met_in[d] for d in range(n_col)]))
    shift = count
    while shift < BLK:
        metric = metric + pltpu.roll(metric, shift, 1)
        shift *= 2
    lines = [jnp.broadcast_to(metric[:, k:k + 1], (count, BLK)) for k in range(count)]
    solved = x_own
    pivots = jnp.ones((count, BLK), F32)
    for k in range(count):
        pivot = lines[k][k:k + 1]
        pivots = jnp.where(sub == k, pivot, pivots)
        ratio = jnp.where(sub == k, 0.0, lines[k] / pivot)
        solved = solved - ratio * solved[k:k + 1]
        for j in range(k + 1, count):
            lines[j] = lines[j] - ratio * lines[j][k:k + 1]
    high, low = halves(solved / pivots)
    y_two = jnp.concatenate(
        [jnp.concatenate([high] * per, axis=0), jnp.concatenate([low] * per, axis=0)], axis=1
    )

    drain(p2_in.at[pl.ds(0, n_row - 1)], p2_r)
    image = own_diag + p2_out[my_row]
    for d in range(n_row - 1):
        image = image + p2_in[d]
    drain(p1_in.at[pl.ds(0, n_col - 1)], p1_r)
    image = add([image, p1_out[my_col]] + [p1_in[d] for d in range(n_col - 1)])
    out_ref[0] = image

    if direct:
        far_sum[...] = jnp.zeros_like(far_sum)

        @pl.when(first)
        def _():
            drain(far_p1, far_r)
            far_left, far_right = [], []
            for row in range(n_row):
                both = jnp.concatenate(halves(col_x[row]), axis=0)
                p_far = jnp.concatenate(halves(far_p1[row]), axis=0)
                far_left += [both, p_far]
                far_right += [p_far, both]
            far_sum[...] = products(far_left, far_right)

        drain(g1_in.at[pl.ds(0, n_row * n_col - 1)], g1_r)
        gram = add([far_sum[...]] + [g1_in[d] for d in range(n_row * n_col)])
    else:
        drain(g2_in.at[pl.ds(0, n_col - 1)], g2_r)
        gram = add([g2_out[...]] + [g2_in[d] for d in range(n_col - 1)])
    wide = unpack(gram)
    o = dot_nn(jnp.concatenate(halves(wide), axis=0), y_two)
    out_ref[1] = image - (o[:count, :BLK] + o[count:, :BLK] + o[:count, BLK:])
    drain(sent, send)
    if direct:
        @pl.when(last)
        def _():
            drain(far_p1.at[pl.ds(0, FAST)], far_s)


def part_kernel(both_ref, image_ref, resid_ref):
    image_ref[...] = both_ref[0]
    resid_ref[...] = both_ref[1]


def per_device(n_row, n_col, vectors, diag_energy, blocks, block_row, block_col):
    count = vectors.shape[0]
    n_blk = blocks.shape[1]
    groups = count // 8
    piece = (count, BLK)
    direct = n_row * n_col <= DIRECT
    n_all = n_row * n_col if direct else n_row
    pieces = 2 * (n_row + n_col - 2)
    small = n_col - 1 + n_all - 1 + (0 if direct else n_col - 1)
    vmem = pl.BlockSpec(memory_space=pltpu.VMEM)
    dma = pltpu.SemaphoreType.DMA
    both = pl.pallas_call(
        functools.partial(kernel, n_row, n_col),
        out_shape=pltpu.VMEM((2,) + piece, F32),
        in_specs=[pl.BlockSpec(memory_space=pl.ANY)] * 5,
        out_specs=vmem,
        scratch_shapes=[
            pltpu.VMEM(piece, F32),
            pltpu.VMEM((1, BLK), F32),
            pltpu.SMEM((1, n_blk), jnp.int32),
            pltpu.SMEM((1, n_blk), jnp.int32),
            pltpu.VMEM((n_blk, BLK, BLK), F32),
            pltpu.VMEM((n_blk, BLK, 2 * BLK), BF16),
            pltpu.VMEM((n_row,) + piece, F32),
            pltpu.VMEM((n_col,) + piece, F32),
            pltpu.VMEM((n_row, 2 * count, 2 * BLK), BF16),
            pltpu.VMEM((n_col, 2 * count, BLK), BF16),
            pltpu.VMEM((n_col, groups, BLK), F32),
            pltpu.VMEM((n_col,) + piece, F32),
            pltpu.VMEM((n_col - 1,) + piece, F32),
            pltpu.VMEM((n_row,) + piece, F32),
            pltpu.VMEM((n_row - 1,) + piece, F32),
            pltpu.VMEM((groups, BLK), F32),
            pltpu.VMEM((n_all, groups, BLK), F32),
            pltpu.VMEM((groups, BLK), F32),
            pltpu.VMEM((n_col, groups, BLK), F32),
            pltpu.VMEM((8 * pieces + small, groups, BLK), F32),
            pltpu.VMEM((n_row,) + piece, F32),
            pltpu.VMEM((groups, BLK), F32),
            pltpu.VMEM((groups, BLK), F32),
            dma((5,)),
            dma, dma, dma((2,)), dma, dma, dma, dma, dma, dma, dma,
        ],
        compiler_params=pltpu.CompilerParams(collective_id=0, has_side_effects=True),
    )(vectors, diag_energy.reshape(1, -1), block_row, block_col, blocks)
    return pl.pallas_call(
        part_kernel,
        out_shape=[jax.ShapeDtypeStruct(piece, F32)] * 2,
        in_specs=[vmem],
        out_specs=[vmem, vmem],
    )(pltpu.with_memory_space_constraint(both, pltpu.VMEM))


def solution(mesh):
    return jax.shard_map(
        functools.partial(per_device, mesh.shape["row"], mesh.shape["col"]),
        mesh=mesh,
        in_specs=(
            P(None, ("row", "col")),
            P(("row", "col")),
            P("row", "col", None, None),
            P("row", "col"),
            P("row", "col"),
        ),
        out_specs=(P(None, ("row", "col")), P(None, ("row", "col"))),
        check_vma=False,
    )
```

```python
import functools

import jax
import jax.numpy as jnp
from jax import lax
from jax.experimental import pallas as pl
from jax.experimental.pallas import tpu as pltpu
from jax.sharding import PartitionSpec as P

BLK = 128
DIRECT = 64
FAST = 2
F32 = jnp.float32
BF16 = jnp.bfloat16
MESH = pl.DeviceIdType.MESH


def halves(x):
    high = x.astype(BF16)
    return high, (x - high.astype(F32)).astype(BF16)


def add(terms):
    while len(terms) > 1:
        terms = [a + b for a, b in zip(terms[::2], terms[1::2])] + terms[len(terms) & ~1:]
    return terms[0]


def dot_nt(a, b):
    return lax.dot_general(a, b, (((1,), (1,)), ((), ())), preferred_element_type=F32)


def dot_nn(a, b):
    return lax.dot_general(a, b, (((1,), (0,)), ((), ())), preferred_element_type=F32)


def drain(ref, sem):
    pltpu.make_async_copy(ref, ref, sem).wait()


def kernel(
    n_row, n_col,
    x_hbm, diag_hbm, rows_hbm, cols_hbm, blocks_hbm,
    out_ref,
    x_ref, diag_ref, rows_ref, cols_ref, tiles, split, col_x, row_x, col_lhs, row_lhs,
    met_in, p1_out, p1_in, p2_out, p2_in, g1_out, g1_in, g2_out, g2_in, sent, far_p1, far_g, far_sum,
    load_sem, send, cx_r, rx_r, m_r, p1_r, p2_r, g1_r, g2_r, far_s, far_r,
):
    count = x_ref.shape[0]
    n_blk = tiles.shape[0]
    my_row = lax.axis_index("row")
    my_col = lax.axis_index("col")
    direct = n_row * n_col <= DIRECT

    last = my_col == n_col - 1
    first = (my_col == 0) & (my_row < FAST)

    def push(source, target, recv, peer, sem=send):
        pltpu.make_async_remote_copy(
            src_ref=source, dst_ref=target, send_sem=sem, recv_sem=recv,
            device_id=peer, device_id_type=MESH,
        ).start()

    def others(size, me):
        return [lax.rem(me + d, size) for d in range(1, size)]

    barrier = pltpu.get_barrier_semaphore()
    for peer in others(n_col, my_col):
        pl.semaphore_signal(barrier, inc=1, device_id={"col": peer}, device_id_type=MESH)
    for peer in others(n_row, my_row):
        pl.semaphore_signal(barrier, inc=1, device_id={"row": peer}, device_id_type=MESH)

    x_load, *small_loads, load = [
        pltpu.make_async_copy(source, target, load_sem.at[at])
        for at, (source, target) in enumerate(
            [(x_hbm, x_ref), (diag_hbm, diag_ref), (rows_hbm, rows_ref), (cols_hbm, cols_ref),
             (blocks_hbm.at[0], tiles)]
        )
    ]
    for copy in [x_load, *small_loads, load]:
        copy.start()
    x_load.wait()
    pl.semaphore_wait(barrier, n_row + n_col - 2)

    mirror = n_col - 1 - my_col
    upper = my_col // (n_col // 2)
    for at in range(1, n_col):
        far = upper * at + (1 - upper) * (n_col - at)
        peer = lax.rem(my_col + far, n_col)
        push(x_ref, row_x.at[my_col], rx_r.at[(peer == mirror).astype(jnp.int32)], {"col": peer})
    for peer in others(n_row, my_row):
        push(x_ref, col_x.at[my_row], cx_r, {"row": peer})
    x_own = x_ref[...]
    row_x[my_col] = x_own
    col_x[my_row] = x_own

    for copy in [*small_loads, load]:
        copy.wait()
    for b in range(n_blk):
        high, low = halves(tiles[b])
        split[b] = jnp.concatenate([high, low], axis=1)

    per = BLK // count
    groups = count // 8
    lane = lax.broadcasted_iota(jnp.int32, (count, BLK), 1)
    sub = lax.broadcasted_iota(jnp.int32, (count, BLK), 0)
    keep = (lane // count) == (sub % per)

    def fold(o):
        return o[:count, :count] + o[count:, :count] + o[:count, count:]

    def pack(square):
        spread = jnp.where(keep, jnp.concatenate([square] * per, axis=1), 0.0)
        return jnp.concatenate(
            [jnp.sum(spread[g * per:(g + 1) * per], axis=0, keepdims=True) for g in range(groups)], axis=0
        )

    def unpack(packed):
        wide = jnp.concatenate(
            [jnp.broadcast_to(packed[g:g + 1], (per, BLK)) for g in range(groups)], axis=0
        )
        return jnp.where(keep, wide, 0.0)

    drain(col_x.at[pl.ds(0, n_row - 1)], cx_r)
    zero = jnp.zeros((count, BLK), BF16)
    col_two = []
    for q in range(n_row):
        high, low = halves(col_x[q])
        col_lhs[q] = jnp.concatenate(
            [jnp.concatenate([high, high], axis=1), jnp.concatenate([low, zero], axis=1)], axis=0
        )
        col_two.append(jnp.concatenate([high, low], axis=0))
    x_wide = jnp.concatenate(col_two, axis=1)
    met_in[my_col] = pack(fold(dot_nt(x_wide, x_wide)))
    for peer in others(n_col, my_col):
        push(met_in.at[my_col], met_in.at[my_col], m_r, {"col": peer})

    part_one = [jnp.zeros((count, BLK), F32) for _ in range(n_col)]
    for b in range(n_blk):
        o = dot_nt(col_lhs[cols_ref[0, b]], split[b])
        term = o[:count] + o[count:]
        place = rows_ref[0, b]
        for r in range(n_col):
            part_one[r] = part_one[r] + (place == r).astype(F32) * term
    for r in range(n_col):
        p1_out[r] = part_one[r]
    if direct:
        @pl.when(last)
        def _():
            for row in range(FAST):
                push(p1_out.at[0], far_p1.at[my_row], far_r, {"row": row, "col": 0}, far_s)
    for d, peer in enumerate(others(n_col, my_col)):
        push(p1_out.at[peer], p1_in.at[d], p1_r, {"col": peer})

    own_diag = diag_ref[...] * x_own
    left = [jnp.concatenate(halves(x_own), axis=0)]
    right = [jnp.concatenate(halves(own_diag), axis=0)]
    order = [lax.rem(mirror + k, n_col) for k in range(1, n_col)] + [mirror]
    p_two = [jnp.concatenate(halves(p1_out[at]), axis=0) for at in order]

    def products(left, right):
        return pack(fold(dot_nt(jnp.concatenate(left, axis=1), jnp.concatenate(right, axis=1))))

    def both_ways(at, p_at):
        both = jnp.concatenate(halves(row_x[at]), axis=0)
        return [both, p_at], [p_at, both]

    def spread_out(ats, me):
        for at in ats:
            to = at + (at >= me).astype(jnp.int32)
            push(
                g1_in.at[me], g1_in.at[me], g1_r,
                {"row": lax.rem(to, n_row), "col": to // n_row},
            )

    me = my_col * n_row + my_row
    drain(row_x.at[pl.ds(0, n_col - 2)], rx_r.at[0])
    if direct:
        @pl.when(last)
        def _():
            some_left, some_right = list(left), list(right)
            for at, p_at in zip(order[:-1], p_two):
                one, two = both_ways(at, p_at)
                some_left += one
                some_right += two
            far_g[...] = products(some_left, some_right)
            for row in range(FAST):
                push(far_g, g1_in.at[me], g1_r, {"row": row, "col": 0})

    drain(row_x.at[pl.ds(0, 1)], rx_r.at[1])
    for at, p_at in zip(order, p_two):
        one, two = both_ways(at, p_at)
        row_lhs[at] = one[0]
        left += one
        right += two
    packed = products(left, right)
    if direct:
        g1_in[me] = packed

        @pl.when(jnp.logical_not(last))
        def _():
            spread_out(range(FAST), me)

        spread_out(range(FAST, n_row * n_col - 1), me)
    else:
        g1_out[...] = packed
        for d, peer in enumerate(others(n_row, my_row)):
            push(g1_out, g1_in.at[d], g1_r, {"row": peer})

    part_two = [jnp.zeros((count, BLK), F32) for _ in range(n_row)]
    for b in range(n_blk):
        o = dot_nn(row_lhs[rows_ref[0, b]], split[b])
        term = o[:count, :BLK] + o[count:, :BLK] + o[:count, BLK:]
        place = cols_ref[0, b]
        for q in range(n_row):
            part_two[q] = part_two[q] + (place == q).astype(F32) * term
    for q in range(n_row):
        p2_out[q] = part_two[q]
    for d, peer in enumerate(others(n_row, my_row)):
        push(p2_out.at[peer], p2_in.at[d], p2_r, {"row": peer})

    if not direct:
        drain(g1_in.at[pl.ds(0, n_row - 1)], g1_r)
        g2_out[...] = add([g1_out[...]] + [g1_in[d] for d in range(n_row - 1)])
        for d, peer in enumerate(others(n_col, my_col)):
            push(g2_out, g2_in.at[d], g2_r, {"col": peer})

    drain(met_in.at[pl.ds(0, n_col - 1)], m_r)
    metric = unpack(add([met_in[d] for d in range(n_col)]))
    shift = count
    while shift < BLK:
        metric = metric + pltpu.roll(metric, shift, 1)
        shift *= 2
    lines = [jnp.broadcast_to(metric[:, k:k + 1], (count, BLK)) for k in range(count)]
    solved = x_own
    pivots = jnp.ones((count, BLK), F32)
    for k in range(count):
        pivot = lines[k][k:k + 1]
        pivots = jnp.where(sub == k, pivot, pivots)
        ratio = jnp.where(sub == k, 0.0, lines[k] / pivot)
        solved = solved - ratio * solved[k:k + 1]
        for j in range(k + 1, count):
            lines[j] = lines[j] - ratio * lines[j][k:k + 1]
    high, low = halves(solved / pivots)
    y_two = jnp.concatenate(
        [jnp.concatenate([high] * per, axis=0), jnp.concatenate([low] * per, axis=0)], axis=1
    )

    drain(p2_in.at[pl.ds(0, n_row - 1)], p2_r)
    image = own_diag + p2_out[my_row]
    for d in range(n_row - 1):
        image = image + p2_in[d]
    drain(p1_in.at[pl.ds(0, n_col - 1)], p1_r)
    image = add([image, p1_out[my_col]] + [p1_in[d] for d in range(n_col - 1)])
    out_ref[0] = image

    if direct:
        far_sum[...] = jnp.zeros_like(far_sum)

        @pl.when(first)
        def _():
            drain(far_p1, far_r)
            far_left, far_right = [], []
            for row in range(n_row):
                both = jnp.concatenate(halves(col_x[row]), axis=0)
                p_far = jnp.concatenate(halves(far_p1[row]), axis=0)
                far_left += [both, p_far]
                far_right += [p_far, both]
            far_sum[...] = products(far_left, far_right)

        drain(g1_in.at[pl.ds(0, n_row * n_col - 1)], g1_r)
        gram = add([far_sum[...]] + [g1_in[d] for d in range(n_row * n_col)])
    else:
        drain(g2_in.at[pl.ds(0, n_col - 1)], g2_r)
        gram = add([g2_out[...]] + [g2_in[d] for d in range(n_col - 1)])
    wide = unpack(gram)
    o = dot_nn(jnp.concatenate(halves(wide), axis=0), y_two)
    out_ref[1] = image - (o[:count, :BLK] + o[count:, :BLK] + o[:count, BLK:])
    drain(sent, send)
    if direct:
        @pl.when(last)
        def _():
            drain(far_p1.at[pl.ds(0, FAST)], far_s)


def part_kernel(both_ref, image_ref, resid_ref):
    image_ref[...] = both_ref[0]
    resid_ref[...] = both_ref[1]


def per_device(n_row, n_col, vectors, diag_energy, blocks, block_row, block_col):
    count = vectors.shape[0]
    n_blk = blocks.shape[1]
    groups = count // 8
    piece = (count, BLK)
    direct = n_row * n_col <= DIRECT
    n_all = n_row * n_col if direct else n_row
    pieces = 2 * (n_row + n_col - 2)
    small = n_col - 1 + n_all - 1 + (0 if direct else n_col - 1)
    vmem = pl.BlockSpec(memory_space=pltpu.VMEM)
    dma = pltpu.SemaphoreType.DMA
    both = pl.pallas_call(
        functools.partial(kernel, n_row, n_col),
        out_shape=pltpu.VMEM((2,) + piece, F32),
        in_specs=[pl.BlockSpec(memory_space=pl.ANY)] * 5,
        out_specs=vmem,
        scratch_shapes=[
            pltpu.VMEM(piece, F32),
            pltpu.VMEM((1, BLK), F32),
            pltpu.SMEM((1, n_blk), jnp.int32),
            pltpu.SMEM((1, n_blk), jnp.int32),
            pltpu.VMEM((n_blk, BLK, BLK), F32),
            pltpu.VMEM((n_blk, BLK, 2 * BLK), BF16),
            pltpu.VMEM((n_row,) + piece, F32),
            pltpu.VMEM((n_col,) + piece, F32),
            pltpu.VMEM((n_row, 2 * count, 2 * BLK), BF16),
            pltpu.VMEM((n_col, 2 * count, BLK), BF16),
            pltpu.VMEM((n_col, groups, BLK), F32),
            pltpu.VMEM((n_col,) + piece, F32),
            pltpu.VMEM((n_col - 1,) + piece, F32),
            pltpu.VMEM((n_row,) + piece, F32),
            pltpu.VMEM((n_row - 1,) + piece, F32),
            pltpu.VMEM((groups, BLK), F32),
            pltpu.VMEM((n_all, groups, BLK), F32),
            pltpu.VMEM((groups, BLK), F32),
            pltpu.VMEM((n_col, groups, BLK), F32),
            pltpu.VMEM((8 * pieces + small, groups, BLK), F32),
            pltpu.VMEM((n_row,) + piece, F32),
            pltpu.VMEM((groups, BLK), F32),
            pltpu.VMEM((groups, BLK), F32),
            dma((5,)),
            dma, dma, dma((2,)), dma, dma, dma, dma, dma, dma, dma,
        ],
        compiler_params=pltpu.CompilerParams(collective_id=0, has_side_effects=True),
    )(vectors, diag_energy.reshape(1, -1), block_row, block_col, blocks)
    return pl.pallas_call(
        part_kernel,
        out_shape=[jax.ShapeDtypeStruct(piece, F32)] * 2,
        in_specs=[vmem],
        out_specs=[vmem, vmem],
    )(pltpu.with_memory_space_constraint(both, pltpu.VMEM))


def solution(mesh):
    return jax.shard_map(
        functools.partial(per_device, mesh.shape["row"], mesh.shape["col"]),
        mesh=mesh,
        in_specs=(
            P(None, ("row", "col")),
            P(("row", "col")),
            P("row", "col", None, None),
            P("row", "col"),
            P("row", "col"),
        ),
        out_specs=(P(None, ("row", "col")), P(None, ("row", "col"))),
        check_vma=False,
    )
```

```python
import functools

import jax
import jax.numpy as jnp
from jax import lax
from jax.experimental import pallas as pl
from jax.experimental.pallas import tpu as pltpu
from jax.sharding import PartitionSpec as P

BLK = 128
DIRECT = 64
FAST = 2
F32 = jnp.float32
BF16 = jnp.bfloat16
MESH = pl.DeviceIdType.MESH


def halves(x):
    high = x.astype(BF16)
    return high, (x - high.astype(F32)).astype(BF16)


def add(terms):
    while len(terms) > 1:
        terms = [a + b for a, b in zip(terms[::2], terms[1::2])] + terms[len(terms) & ~1:]
    return terms[0]


def dot_nt(a, b):
    return lax.dot_general(a, b, (((1,), (1,)), ((), ())), preferred_element_type=F32)


def dot_nn(a, b):
    return lax.dot_general(a, b, (((1,), (0,)), ((), ())), preferred_element_type=F32)


def drain(ref, sem):
    pltpu.make_async_copy(ref, ref, sem).wait()


def kernel(
    n_row, n_col,
    x_hbm, diag_hbm, rows_hbm, cols_hbm, blocks_hbm,
    out_ref,
    x_ref, diag_ref, rows_ref, cols_ref, tiles, split, col_x, row_x, col_lhs, row_lhs,
    met_in, p1_out, p2_out, p_in, g1_out, g1_in, g2_out, g2_in, sent, far_p1, far_g, far_sum,
    load_sem, cx_r, rx_r, m_r, p_r, g1_r, far_r, *g2_r,
):
    count = x_ref.shape[0]
    n_blk = tiles.shape[0]
    my_row = lax.axis_index("row")
    my_col = lax.axis_index("col")
    direct = n_row * n_col <= DIRECT

    send, far_s = load_sem.at[0], load_sem.at[1]
    last = my_col == n_col - 1
    first = (my_col == 0) & (my_row < FAST)

    def push(source, target, recv, peer, sem=send):
        pltpu.make_async_remote_copy(
            src_ref=source, dst_ref=target, send_sem=sem, recv_sem=recv,
            device_id=peer, device_id_type=MESH,
        ).start()

    def others(size, me):
        return [lax.rem(me + d, size) for d in range(1, size)]

    barrier = pltpu.get_barrier_semaphore()
    for peer in others(n_col, my_col):
        pl.semaphore_signal(barrier, inc=1, device_id={"col": peer}, device_id_type=MESH)
    for peer in others(n_row, my_row):
        pl.semaphore_signal(barrier, inc=1, device_id={"row": peer}, device_id_type=MESH)

    x_load, *small_loads, load = [
        pltpu.make_async_copy(source, target, load_sem.at[at])
        for at, (source, target) in enumerate(
            [(x_hbm, x_ref), (diag_hbm, diag_ref), (rows_hbm, rows_ref), (cols_hbm, cols_ref),
             (blocks_hbm.at[0], tiles)]
        )
    ]
    for copy in [x_load, *small_loads, load]:
        copy.start()
    x_load.wait()
    pl.semaphore_wait(barrier, n_row + n_col - 2)

    mirror = n_col - 1 - my_col
    half = n_col // 2
    upper = my_col // half
    skip = (my_col == 0).astype(jnp.int32)
    for at in range(n_col - 1):
        if at < half:
            peer = upper * at + (1 - upper) * (n_col - 1 - lax.rem(at + skip, half))
        else:
            peer = upper * half + lax.rem(my_col + 1 + at - half, half)
        push(x_ref, row_x.at[my_col], rx_r.at[(0 if at >= half else 1) + (peer == mirror).astype(jnp.int32)], {"col": peer})
    for peer in others(n_row, my_row):
        push(x_ref, col_x.at[my_row], cx_r, {"row": peer})
    x_own = x_ref[...]
    row_x[my_col] = x_own
    col_x[my_row] = x_own

    for copy in [*small_loads, load]:
        copy.wait()
    for b in range(n_blk):
        high, low = halves(tiles[b])
        split[b] = jnp.concatenate([high, low], axis=1)

    per = BLK // count
    groups = count // 8
    lane = lax.broadcasted_iota(jnp.int32, (count, BLK), 1)
    sub = lax.broadcasted_iota(jnp.int32, (count, BLK), 0)
    keep = (lane // count) == (sub % per)

    def pack(o):
        wide = jnp.concatenate([o[:count], jnp.zeros((count, BLK - 2 * count), F32)], axis=1)
        wide = wide + jnp.concatenate([o[count:, :count], jnp.zeros((count, BLK - count), F32)], axis=1)
        spread = add([wide] + [pltpu.roll(wide, count * at, 1) for at in range(1, per)])
        spread = jnp.where(keep, spread, 0.0)
        return jnp.concatenate(
            [jnp.sum(spread[g * per:(g + 1) * per], axis=0, keepdims=True) for g in range(groups)], axis=0
        )

    def unpack(packed):
        wide = jnp.concatenate(
            [jnp.broadcast_to(packed[g:g + 1], (per, BLK)) for g in range(groups)], axis=0
        )
        return jnp.where(keep, wide, 0.0)

    drain(col_x.at[pl.ds(0, n_row - 1)], cx_r)
    zero = jnp.zeros((count, BLK), BF16)
    col_two = []
    for q in range(n_row):
        high, low = halves(col_x[q])
        col_lhs[q] = jnp.concatenate(
            [jnp.concatenate([high, high], axis=1), jnp.concatenate([low, zero], axis=1)], axis=0
        )
        col_two.append(jnp.concatenate([high, low], axis=0))
    x_wide = jnp.concatenate(col_two, axis=1)
    met_in[my_col] = pack((dot_nt(x_wide, x_wide)))

    part_one = [jnp.zeros((count, BLK), F32) for _ in range(n_col)]
    for b in range(n_blk):
        if b == n_blk // 3:
            for peer in others(n_col, my_col):
                push(met_in.at[my_col], met_in.at[my_col], m_r, {"col": peer})
        o = dot_nt(col_lhs[cols_ref[0, b]], split[b])
        term = o[:count] + o[count:]
        place = rows_ref[0, b]
        for r in range(n_col):
            part_one[r] = part_one[r] + (place == r).astype(F32) * term
    for r in range(n_col):
        p1_out[r] = part_one[r]
    if direct:
        @pl.when(last)
        def _():
            for row in range(FAST):
                push(p1_out.at[0], far_p1.at[my_row], far_r, {"row": row, "col": 0}, far_s)
    for d, peer in enumerate(others(n_col, my_col)):
        push(p1_out.at[peer], p_in.at[d], p_r, {"col": peer})

    own_diag = diag_ref[...] * x_own
    left = [jnp.concatenate(halves(x_own), axis=0)]
    right = [jnp.concatenate(halves(own_diag), axis=0)]
    near = [upper * half + at for at in range(half)]
    far = [(1 - upper) * half + lax.rem(mirror + at, half) for at in range(1, half)]
    order = near + far + [mirror]
    p_two = [jnp.concatenate(halves(p1_out[at]), axis=0) for at in order]

    def products(left, right):
        return dot_nt(jnp.concatenate(left, axis=1), jnp.concatenate(right, axis=1))

    def spread_out(ats, me):
        for at in ats:
            to = at + (at >= me).astype(jnp.int32)
            push(
                g1_in.at[me], g1_in.at[me], g1_r,
                {"row": lax.rem(to, n_row), "col": to // n_row},
            )

    me = my_col * n_row + my_row
    def gathered(some):
        left, right = [], []
        for at, p_at in some:
            both = jnp.concatenate(halves(row_x[at]), axis=0)
            left += [both, p_at]
            right += [p_at, both]
        return left, right

    pairs = list(zip(order, p_two))
    drain(row_x.at[pl.ds(0, half - 1)], rx_r.at[0])
    one, two = gathered(pairs[:half])
    near_sum = products(left + one, right + two)
    for at, both in zip(near, one[::2]):
        row_lhs[at] = both
    drain(row_x.at[pl.ds(0, half - 1)], rx_r.at[1])
    if direct:
        @pl.when(last)
        def _():
            far_g[...] = pack(near_sum + products(*gathered(pairs[half:-1])))
            for row in range(FAST):
                push(far_g, g1_in.at[me], g1_r, {"row": row, "col": 0})

    drain(row_x.at[pl.ds(0, 1)], rx_r.at[2])
    one, two = gathered(pairs[half:])
    packed = pack(near_sum + products(one, two))
    if direct:
        g1_in[me] = packed

        @pl.when(jnp.logical_not(last))
        def _():
            spread_out(range(FAST), me)

        spread_out(range(FAST, n_row * n_col - 1), me)
    else:
        g1_out[...] = packed
        for d, peer in enumerate(others(n_row, my_row)):
            push(g1_out, g1_in.at[d], g1_r, {"row": peer})

    for at, both in zip(order[half:], one[::2]):
        row_lhs[at] = both

    part_two = [jnp.zeros((count, BLK), F32) for _ in range(n_row)]
    for b in range(n_blk):
        o = dot_nn(row_lhs[rows_ref[0, b]], split[b])
        term = o[:count, :BLK] + o[count:, :BLK] + o[:count, BLK:]
        place = cols_ref[0, b]
        for q in range(n_row):
            part_two[q] = part_two[q] + (place == q).astype(F32) * term
    for q in range(n_row):
        p2_out[q] = part_two[q]
    for d, peer in enumerate(others(n_row, my_row)):
        push(p2_out.at[peer], p_in.at[n_col - 1 + d], p_r, {"row": peer})

    if not direct:
        drain(g1_in.at[pl.ds(0, n_row - 1)], g1_r)
        g2_out[...] = add([g1_out[...]] + [g1_in[d] for d in range(n_row - 1)])
        for d, peer in enumerate(others(n_col, my_col)):
            push(g2_out, g2_in.at[d], g2_r[0], {"col": peer})

    drain(met_in.at[pl.ds(0, n_col - 1)], m_r)
    metric = unpack(add([met_in[d] for d in range(n_col)]))
    shift = count
    while shift < BLK:
        metric = metric + pltpu.roll(metric, shift, 1)
        shift *= 2
    lines = [jnp.broadcast_to(metric[:, k:k + 1], (count, BLK)) for k in range(count)]
    solved = x_own
    pivots = jnp.ones((count, BLK), F32)
    for k in range(count):
        pivot = lines[k][k:k + 1]
        pivots = jnp.where(sub == k, pivot, pivots)
        ratio = jnp.where(sub == k, 0.0, lines[k] / pivot)
        solved = solved - ratio * solved[k:k + 1]
        for j in range(k + 1, count):
            lines[j] = lines[j] - ratio * lines[j][k:k + 1]
    high, low = halves(solved / pivots)
    y_two = jnp.concatenate(
        [jnp.concatenate([high] * per, axis=0), jnp.concatenate([low] * per, axis=0)], axis=1
    )

    drain(p_in, p_r)
    image = own_diag + p2_out[my_row]
    for d in range(n_row - 1):
        image = image + p_in[n_col - 1 + d]
    image = add([image, p1_out[my_col]] + [p_in[d] for d in range(n_col - 1)])
    out_ref[0] = image

    if direct:
        far_sum[...] = jnp.zeros_like(far_sum)

        @pl.when(first)
        def _():
            drain(far_p1, far_r)
            far_left, far_right = [], []
            for row in range(n_row):
                both = jnp.concatenate(halves(col_x[row]), axis=0)
                p_far = jnp.concatenate(halves(far_p1[row]), axis=0)
                far_left += [both, p_far]
                far_right += [p_far, both]
            far_sum[...] = pack(products(far_left, far_right))

        drain(g1_in.at[pl.ds(0, n_row * n_col - 1)], g1_r)
        gram = add([far_sum[...]] + [g1_in[d] for d in range(n_row * n_col)])
    else:
        drain(g2_in.at[pl.ds(0, n_col - 1)], g2_r[0])
        gram = add([g2_out[...]] + [g2_in[d] for d in range(n_col - 1)])
    wide = unpack(gram)
    o = dot_nn(jnp.concatenate(halves(wide), axis=0), y_two)
    out_ref[1] = image - (o[:count, :BLK] + o[count:, :BLK] + o[:count, BLK:])
    drain(sent, send)
    if direct:
        @pl.when(last)
        def _():
            drain(far_p1.at[pl.ds(0, FAST)], far_s)


def part_kernel(both_ref, image_ref, resid_ref):
    image_ref[...] = both_ref[0]
    resid_ref[...] = both_ref[1]


def per_device(n_row, n_col, vectors, diag_energy, blocks, block_row, block_col):
    count = vectors.shape[0]
    n_blk = blocks.shape[1]
    groups = count // 8
    piece = (count, BLK)
    direct = n_row * n_col <= DIRECT
    n_all = n_row * n_col if direct else n_row
    pieces = 2 * (n_row + n_col - 2)
    small = n_col - 1 + n_all - 1 + (0 if direct else n_col - 1)
    vmem = pl.BlockSpec(memory_space=pltpu.VMEM)
    dma = pltpu.SemaphoreType.DMA
    both = pl.pallas_call(
        functools.partial(kernel, n_row, n_col),
        out_shape=pltpu.VMEM((2,) + piece, F32),
        in_specs=[pl.BlockSpec(memory_space=pl.ANY)] * 5,
        out_specs=vmem,
        scratch_shapes=[
            pltpu.VMEM(piece, F32),
            pltpu.VMEM((1, BLK), F32),
            pltpu.SMEM((1, n_blk), jnp.int32),
            pltpu.SMEM((1, n_blk), jnp.int32),
            pltpu.VMEM((n_blk, BLK, BLK), F32),
            pltpu.VMEM((n_blk, BLK, 2 * BLK), BF16),
            pltpu.VMEM((n_row,) + piece, F32),
            pltpu.VMEM((n_col,) + piece, F32),
            pltpu.VMEM((n_row, 2 * count, 2 * BLK), BF16),
            pltpu.VMEM((n_col, 2 * count, BLK), BF16),
            pltpu.VMEM((n_col, groups, BLK), F32),
            pltpu.VMEM((n_col,) + piece, F32),
            pltpu.VMEM((n_row,) + piece, F32),
            pltpu.VMEM((n_col + n_row - 2,) + piece, F32),
            pltpu.VMEM((groups, BLK), F32),
            pltpu.VMEM((n_all, groups, BLK), F32),
            pltpu.VMEM((groups, BLK), F32),
            pltpu.VMEM((n_col, groups, BLK), F32),
            pltpu.VMEM((8 * pieces + small, groups, BLK), F32),
            pltpu.VMEM((n_row,) + piece, F32),
            pltpu.VMEM((groups, BLK), F32),
            pltpu.VMEM((groups, BLK), F32),
            dma((5,)),
            dma, dma((3,)), dma, dma, dma, dma,
            *([] if direct else [dma]),
        ],
        compiler_params=pltpu.CompilerParams(collective_id=0, has_side_effects=True),
    )(vectors, diag_energy.reshape(1, -1), block_row, block_col, blocks)
    return pl.pallas_call(
        part_kernel,
        out_shape=[jax.ShapeDtypeStruct(piece, F32)] * 2,
        in_specs=[vmem],
        out_specs=[vmem, vmem],
    )(pltpu.with_memory_space_constraint(both, pltpu.VMEM))


def solution(mesh):
    return jax.shard_map(
        functools.partial(per_device, mesh.shape["row"], mesh.shape["col"]),
        mesh=mesh,
        in_specs=(
            P(None, ("row", "col")),
            P(("row", "col")),
            P("row", "col", None, None),
            P("row", "col"),
            P("row", "col"),
        ),
        out_specs=(P(None, ("row", "col")), P(None, ("row", "col"))),
        check_vma=False,
    )
```

```python
import functools

import jax
import jax.numpy as jnp
from jax import lax
from jax.experimental import pallas as pl
from jax.experimental.pallas import tpu as pltpu
from jax.sharding import PartitionSpec as P

BLK = 128
DIRECT = 64
FAST = 2
F32 = jnp.float32
BF16 = jnp.bfloat16
MESH = pl.DeviceIdType.MESH


def halves(x):
    high = x.astype(BF16)
    return high, (x - high.astype(F32)).astype(BF16)


def add(terms):
    while len(terms) > 1:
        terms = [a + b for a, b in zip(terms[::2], terms[1::2])] + terms[len(terms) & ~1:]
    return terms[0]


def dot_nt(a, b):
    return lax.dot_general(a, b, (((1,), (1,)), ((), ())), preferred_element_type=F32)


def dot_nn(a, b):
    return lax.dot_general(a, b, (((1,), (0,)), ((), ())), preferred_element_type=F32)


def drain(ref, sem):
    pltpu.make_async_copy(ref, ref, sem).wait()


def kernel(
    n_row, n_col,
    x_hbm, diag_hbm, rows_hbm, cols_hbm, blocks_hbm,
    out_ref,
    own, where, tiles, split, col_x, row_x, col_lhs, row_lhs,
    met_in, p1_out, p2_out, p_in, g1_out, g1_in, g2_out, g2_in, sent, far_p1, far_g, far_sum,
    load_sem, cx_r, rx_r, m_r, p_r, g1_r, far_r, *g2_r,
):
    count = x_hbm.shape[0]
    x_ref = own.at[pl.ds(0, count)]
    n_blk = tiles.shape[0]
    my_row = lax.axis_index("row")
    my_col = lax.axis_index("col")
    direct = n_row * n_col <= DIRECT

    send, far_s = load_sem.at[0], load_sem.at[1]
    last = my_col == n_col - 1
    first = (my_col == 0) & (my_row < FAST)

    def push(source, target, recv, peer, sem=send):
        pltpu.make_async_remote_copy(
            src_ref=source, dst_ref=target, send_sem=sem, recv_sem=recv,
            device_id=peer, device_id_type=MESH,
        ).start()

    def others(size, me):
        if size & (size - 1):
            return [lax.rem(me + d, size) for d in range(1, size)]
        return [(me + d) & (size - 1) for d in range(1, size)]

    barrier = pltpu.get_barrier_semaphore()
    for peer in others(n_row, my_row):
        pl.semaphore_signal(barrier, inc=1, device_id={"row": peer}, device_id_type=MESH)
    for peer in others(n_col, my_col):
        pl.semaphore_signal(barrier, inc=1, device_id={"col": peer}, device_id_type=MESH)

    for source, target, at in [
        (x_hbm, x_ref, 0), (diag_hbm, own.at[pl.ds(count, 1)], 0),
        (rows_hbm, where.at[pl.ds(0, 1)], 1), (cols_hbm, where.at[pl.ds(1, 1)], 1), (blocks_hbm.at[0], tiles, 2),
    ]:
        pltpu.make_async_copy(source, target, load_sem.at[at]).start()
    drain(own.at[pl.ds(0, count + 1)], load_sem.at[0])
    pl.semaphore_wait(barrier, n_row + n_col - 2)

    mirror = n_col - 1 - my_col
    half = n_col // 2
    upper = my_col // half
    skip = (my_col == 0).astype(jnp.int32)
    for at in range(n_col - 1):
        if at < half:
            peer = upper * at + (1 - upper) * (n_col - 1 - lax.rem(at + skip, half))
        else:
            peer = upper * half + lax.rem(my_col + 1 + at - half, half)
        push(x_ref, row_x.at[my_col], rx_r.at[(0 if at >= half else 1) + (peer == mirror).astype(jnp.int32)], {"col": peer})
    for peer in others(n_row, my_row):
        push(x_ref, col_x.at[my_row], cx_r, {"row": peer})
    x_own = x_ref[...]
    row_x[my_col] = x_own
    col_x[my_row] = x_own

    drain(where, load_sem.at[1])
    drain(tiles, load_sem.at[2])
    for b in range(n_blk):
        high, low = halves(tiles[b])
        split[b] = jnp.concatenate([high, low], axis=1)

    per = BLK // count
    groups = count // 8
    lane = lax.broadcasted_iota(jnp.int32, (count, BLK), 1)
    sub = lax.broadcasted_iota(jnp.int32, (count, BLK), 0)
    keep = (lane // count) == (sub % per)

    def pack(o):
        wide = jnp.concatenate([o[:count], jnp.zeros((count, BLK - 2 * count), F32)], axis=1)
        wide = wide + jnp.concatenate([o[count:, :count], jnp.zeros((count, BLK - count), F32)], axis=1)
        spread = add([wide] + [pltpu.roll(wide, count * at, 1) for at in range(1, per)])
        spread = jnp.where(keep, spread, 0.0)
        return jnp.concatenate(
            [jnp.sum(spread[g * per:(g + 1) * per], axis=0, keepdims=True) for g in range(groups)], axis=0
        )

    def unpack(packed):
        wide = jnp.concatenate(
            [jnp.broadcast_to(packed[g:g + 1], (per, BLK)) for g in range(groups)], axis=0
        )
        return jnp.where(keep, wide, 0.0)

    drain(col_x.at[pl.ds(0, n_row - 1)], cx_r)
    zero = jnp.zeros((count, BLK), BF16)
    col_two = []
    for q in range(n_row):
        high, low = halves(col_x[q])
        col_lhs[q] = jnp.concatenate(
            [jnp.concatenate([high, high], axis=1), jnp.concatenate([low, zero], axis=1)], axis=0
        )
        col_two.append(jnp.concatenate([high, low], axis=0))
    x_wide = jnp.concatenate(col_two, axis=1)
    met_in[my_col] = pack((dot_nt(x_wide, x_wide)))

    part_one = [jnp.zeros((count, BLK), F32) for _ in range(n_col)]
    for b in range(n_blk):
        if b == n_blk // 3:
            for peer in others(n_col, my_col):
                push(met_in.at[my_col], met_in.at[my_col], m_r, {"col": peer})
        o = dot_nt(col_lhs[where[1, b]], split[b])
        term = o[:count] + o[count:]
        place = where[0, b]
        for r in range(n_col):
            part_one[r] = part_one[r] + (place == r).astype(F32) * term
    for r in range(n_col):
        p1_out[r] = part_one[r]
    if direct:
        @pl.when(last)
        def _():
            for row in range(FAST):
                push(p1_out.at[0], far_p1.at[my_row], far_r, {"row": row, "col": 0}, far_s)
    for d, peer in enumerate(others(n_col, my_col)):
        push(p1_out.at[peer], p_in.at[d], p_r, {"col": peer})

    own_diag = own[count:count + 1] * x_own
    left = [jnp.concatenate(halves(x_own), axis=0)]
    right = [jnp.concatenate(halves(own_diag), axis=0)]
    near = [upper * half + at for at in range(half)]
    far = [(1 - upper) * half + lax.rem(mirror + at, half) for at in range(1, half)]
    order = near + far + [mirror]
    p_two = [jnp.concatenate(halves(p1_out[at]), axis=0) for at in order]

    def products(left, right):
        return dot_nt(jnp.concatenate(left, axis=1), jnp.concatenate(right, axis=1))

    def spread_out(ats, me):
        for at in ats:
            to = at + (at >= me).astype(jnp.int32)
            push(
                g1_in.at[me], g1_in.at[me], g1_r,
                {"row": lax.rem(to, n_row), "col": to // n_row},
            )

    me = my_col * n_row + my_row
    def gathered(some):
        left, right = [], []
        for at, p_at in some:
            both = jnp.concatenate(halves(row_x[at]), axis=0)
            left += [both, p_at]
            right += [p_at, both]
        return left, right

    pairs = list(zip(order, p_two))
    drain(row_x.at[pl.ds(0, half - 1)], rx_r.at[0])
    one, two = gathered(pairs[:half])
    near_sum = products(left + one, right + two)
    for at, both in zip(near, one[::2]):
        row_lhs[at] = both
    drain(row_x.at[pl.ds(0, half - 1)], rx_r.at[1])
    if direct:
        @pl.when(last)
        def _():
            far_g[...] = pack(near_sum + products(*gathered(pairs[half:-1])))
            for row in range(FAST):
                push(far_g, g1_in.at[me], g1_r, {"row": row, "col": 0})

    drain(row_x.at[pl.ds(0, 1)], rx_r.at[2])
    one, two = gathered(pairs[half:])
    packed = pack(near_sum + products(one, two))
    if direct:
        g1_in[me] = packed

        @pl.when(jnp.logical_not(last))
        def _():
            spread_out(range(FAST), me)

        spread_out(range(FAST, n_row * n_col - 1), me)
    else:
        g1_out[...] = packed
        for d, peer in enumerate(others(n_row, my_row)):
            push(g1_out, g1_in.at[d], g1_r, {"row": peer})

    for at, both in zip(order[half:], one[::2]):
        row_lhs[at] = both

    part_two = [jnp.zeros((count, BLK), F32) for _ in range(n_row)]
    for b in range(n_blk):
        o = dot_nn(row_lhs[where[0, b]], split[b])
        term = o[:count, :BLK] + o[count:, :BLK] + o[:count, BLK:]
        place = where[1, b]
        for q in range(n_row):
            part_two[q] = part_two[q] + (place == q).astype(F32) * term
    for q in range(n_row):
        p2_out[q] = part_two[q]
    for d, peer in enumerate(others(n_row, my_row)):
        push(p2_out.at[peer], p_in.at[n_col - 1 + d], p_r, {"row": peer})

    if not direct:
        drain(g1_in.at[pl.ds(0, n_row - 1)], g1_r)
        g2_out[...] = add([g1_out[...]] + [g1_in[d] for d in range(n_row - 1)])
        for d, peer in enumerate(others(n_col, my_col)):
            push(g2_out, g2_in.at[d], g2_r[0], {"col": peer})

    drain(met_in.at[pl.ds(0, n_col - 1)], m_r)
    metric = unpack(add([met_in[d] for d in range(n_col)]))
    shift = count
    while shift < BLK:
        metric = metric + pltpu.roll(metric, shift, 1)
        shift *= 2
    lines = [jnp.broadcast_to(metric[:, k:k + 1], (count, BLK)) for k in range(count)]
    solved = x_own
    pivots = jnp.ones((count, BLK), F32)
    for k in range(count):
        pivot = lines[k][k:k + 1]
        pivots = jnp.where(sub == k, pivot, pivots)
        ratio = jnp.where(sub == k, 0.0, lines[k] / pivot)
        solved = solved - ratio * solved[k:k + 1]
        for j in range(k + 1, count):
            lines[j] = lines[j] - ratio * lines[j][k:k + 1]
    high, low = halves(solved / pivots)
    y_two = jnp.concatenate(
        [jnp.concatenate([high] * per, axis=0), jnp.concatenate([low] * per, axis=0)], axis=1
    )

    drain(p_in, p_r)
    image = own_diag + p2_out[my_row]
    for d in range(n_row - 1):
        image = image + p_in[n_col - 1 + d]
    image = add([image, p1_out[my_col]] + [p_in[d] for d in range(n_col - 1)])
    out_ref[0] = image

    if direct:
        far_sum[...] = jnp.zeros_like(far_sum)

        @pl.when(first)
        def _():
            col_both = [jnp.concatenate(halves(col_x[row]), axis=0) for row in range(n_row)]
            drain(far_p1, far_r)
            far_left, far_right = [], []
            for row, both in enumerate(col_both):
                p_far = jnp.concatenate(halves(far_p1[row]), axis=0)
                far_left += [both, p_far]
                far_right += [p_far, both]
            far_sum[...] = pack(products(far_left, far_right))

        drain(g1_in.at[pl.ds(0, n_row * n_col - 1)], g1_r)
        gram = add([far_sum[...]] + [g1_in[d] for d in range(n_row * n_col)])
    else:
        drain(g2_in.at[pl.ds(0, n_col - 1)], g2_r[0])
        gram = add([g2_out[...]] + [g2_in[d] for d in range(n_col - 1)])
    wide = unpack(gram)
    o = dot_nn(jnp.concatenate(halves(wide), axis=0), y_two)
    out_ref[1] = image - (o[:count, :BLK] + o[count:, :BLK] + o[:count, BLK:])
    drain(sent, send)
    if direct:
        @pl.when(last)
        def _():
            drain(far_p1.at[pl.ds(0, FAST)], far_s)


def part_kernel(both_ref, image_ref, resid_ref):
    image_ref[...] = both_ref[0]
    resid_ref[...] = both_ref[1]


def per_device(n_row, n_col, vectors, diag_energy, blocks, block_row, block_col):
    count = vectors.shape[0]
    n_blk = blocks.shape[1]
    groups = count // 8
    piece = (count, BLK)
    direct = n_row * n_col <= DIRECT
    n_all = n_row * n_col if direct else n_row
    pieces = 2 * (n_row + n_col - 2)
    small = n_col - 1 + n_all - 1 + (0 if direct else n_col - 1)
    vmem = pl.BlockSpec(memory_space=pltpu.VMEM)
    dma = pltpu.SemaphoreType.DMA
    both = pl.pallas_call(
        functools.partial(kernel, n_row, n_col),
        out_shape=pltpu.VMEM((2,) + piece, F32),
        in_specs=[pl.BlockSpec(memory_space=pl.ANY)] * 5,
        out_specs=vmem,
        scratch_shapes=[
            pltpu.VMEM((count + 8, BLK), F32),
            pltpu.SMEM((2, n_blk), jnp.int32),
            pltpu.VMEM((n_blk, BLK, BLK), F32),
            pltpu.VMEM((n_blk, BLK, 2 * BLK), BF16),
            pltpu.VMEM((n_row,) + piece, F32),
            pltpu.VMEM((n_col,) + piece, F32),
            pltpu.VMEM((n_row, 2 * count, 2 * BLK), BF16),
            pltpu.VMEM((n_col, 2 * count, BLK), BF16),
            pltpu.VMEM((n_col, groups, BLK), F32),
            pltpu.VMEM((n_col,) + piece, F32),
            pltpu.VMEM((n_row,) + piece, F32),
            pltpu.VMEM((n_col + n_row - 2,) + piece, F32),
            pltpu.VMEM((groups, BLK), F32),
            pltpu.VMEM((n_all, groups, BLK), F32),
            pltpu.VMEM((groups, BLK), F32),
            pltpu.VMEM((n_col, groups, BLK), F32),
            pltpu.VMEM((8 * pieces + small, groups, BLK), F32),
            pltpu.VMEM((n_row,) + piece, F32),
            pltpu.VMEM((groups, BLK), F32),
            pltpu.VMEM((groups, BLK), F32),
            dma((3,)),
            dma, dma((3,)), dma, dma, dma, dma,
            *([] if direct else [dma]),
        ],
        compiler_params=pltpu.CompilerParams(collective_id=0, has_side_effects=True),
    )(vectors, diag_energy.reshape(1, -1), block_row, block_col, blocks)
    return pl.pallas_call(
        part_kernel,
        out_shape=[jax.ShapeDtypeStruct(piece, F32)] * 2,
        in_specs=[vmem],
        out_specs=[vmem, vmem],
    )(pltpu.with_memory_space_constraint(both, pltpu.VMEM))


def solution(mesh):
    return jax.shard_map(
        functools.partial(per_device, mesh.shape["row"], mesh.shape["col"]),
        mesh=mesh,
        in_specs=(
            P(None, ("row", "col")),
            P(("row", "col")),
            P("row", "col", None, None),
            P("row", "col"),
            P("row", "col"),
        ),
        out_specs=(P(None, ("row", "col")), P(None, ("row", "col"))),
        check_vma=False,
    )
```

```python
import functools

import jax
import jax.numpy as jnp
from jax import lax
from jax.experimental import pallas as pl
from jax.experimental.pallas import tpu as pltpu
from jax.sharding import PartitionSpec as P

BLK = 128
DIRECT = 64
FAST = 2
F32 = jnp.float32
BF16 = jnp.bfloat16
MESH = pl.DeviceIdType.MESH


def halves(x):
    high = x.astype(BF16)
    return high, (x - high.astype(F32)).astype(BF16)


def add(terms):
    while len(terms) > 1:
        terms = [a + b for a, b in zip(terms[::2], terms[1::2])] + terms[len(terms) & ~1:]
    return terms[0]


def dot_nt(a, b):
    return lax.dot_general(a, b, (((1,), (1,)), ((), ())), preferred_element_type=F32)


def dot_nn(a, b):
    return lax.dot_general(a, b, (((1,), (0,)), ((), ())), preferred_element_type=F32)


def drain(ref, sem):
    pltpu.make_async_copy(ref, ref, sem).wait()


def kernel(
    n_row, n_col,
    x_hbm, diag_hbm, rows_hbm, cols_hbm, blocks_hbm,
    out_ref,
    own, where, tiles, split, col_x, row_x, col_lhs, row_lhs,
    met_in, p1_out, p2_out, p_in, g1_out, g1_in, g2_out, g2_in, sent, far_p1, far_g, far_sum,
    load_sem, cx_r, rx_r, m_r, p_r, g1_r, far_r, *g2_r,
):
    count = x_hbm.shape[0]
    x_ref = own.at[pl.ds(0, count)]
    n_blk = tiles.shape[0]
    my_row = lax.axis_index("row")
    my_col = lax.axis_index("col")
    direct = n_row * n_col <= DIRECT

    send, far_s = load_sem.at[0], load_sem.at[1]
    last = my_col == n_col - 1
    first = (my_col == 0) & (my_row < FAST)

    def push(source, target, recv, peer, sem=send):
        pltpu.make_async_remote_copy(
            src_ref=source, dst_ref=target, send_sem=sem, recv_sem=recv,
            device_id=peer, device_id_type=MESH,
        ).start()

    def others(size, me):
        if size & (size - 1):
            return [lax.rem(me + d, size) for d in range(1, size)]
        return [(me + d) & (size - 1) for d in range(1, size)]

    barrier = pltpu.get_barrier_semaphore()
    for peer in others(n_row, my_row):
        pl.semaphore_signal(barrier, inc=1, device_id={"row": peer}, device_id_type=MESH)
    for peer in others(n_col, my_col):
        pl.semaphore_signal(barrier, inc=1, device_id={"col": peer}, device_id_type=MESH)

    for source, target, at in [
        (x_hbm, x_ref, 0), (diag_hbm, own.at[pl.ds(count, 1)], 0),
        (rows_hbm, where.at[pl.ds(0, 1)], 1), (cols_hbm, where.at[pl.ds(1, 1)], 1), (blocks_hbm.at[0], tiles, 2),
    ]:
        pltpu.make_async_copy(source, target, load_sem.at[at]).start()
    drain(own.at[pl.ds(0, count + 1)], load_sem.at[0])
    mirror = n_col - 1 - my_col
    half = n_col // 2
    upper = (my_col >= half).astype(jnp.int32)
    skip = (my_col == 0).astype(jnp.int32)
    base, step = (n_col - 1) * (1 - upper) - skip, 2 * upper - 1
    across = [base + step * at for at in range(half - 1)] + [base + step * (half - 1) + half * skip]
    beside = [upper * half + ((my_col + at) & (half - 1)) for at in range(1, half)]
    pl.semaphore_wait(barrier, n_row + n_col - 2)

    for peer in across:
        push(x_ref, row_x.at[my_col], rx_r.at[1 + (peer == mirror).astype(jnp.int32)], {"col": peer})
    for peer in beside:
        push(x_ref, row_x.at[my_col], rx_r.at[0], {"col": peer})
    for peer in others(n_row, my_row):
        push(x_ref, col_x.at[my_row], cx_r, {"row": peer})
    x_own = x_ref[...]
    row_x[my_col] = x_own
    col_x[my_row] = x_own

    drain(where, load_sem.at[1])
    drain(tiles, load_sem.at[2])
    for b in range(n_blk):
        high, low = halves(tiles[b])
        split[b] = jnp.concatenate([high, low], axis=1)

    per = BLK // count
    groups = count // 8
    lane = lax.broadcasted_iota(jnp.int32, (count, BLK), 1)
    sub = lax.broadcasted_iota(jnp.int32, (count, BLK), 0)
    keep = (lane // count) == (sub % per)

    def pack(o):
        wide = jnp.concatenate([o[:count], jnp.zeros((count, BLK - 2 * count), F32)], axis=1)
        wide = wide + jnp.concatenate([o[count:, :count], jnp.zeros((count, BLK - count), F32)], axis=1)
        spread = add([wide] + [pltpu.roll(wide, count * at, 1) for at in range(1, per)])
        spread = jnp.where(keep, spread, 0.0)
        return jnp.concatenate(
            [jnp.sum(spread[g * per:(g + 1) * per], axis=0, keepdims=True) for g in range(groups)], axis=0
        )

    def unpack(packed):
        wide = jnp.concatenate(
            [jnp.broadcast_to(packed[g:g + 1], (per, BLK)) for g in range(groups)], axis=0
        )
        return jnp.where(keep, wide, 0.0)

    drain(col_x.at[pl.ds(0, n_row - 1)], cx_r)
    zero = jnp.zeros((count, BLK), BF16)
    col_two = []
    for q in range(n_row):
        high, low = halves(col_x[q])
        col_lhs[q] = jnp.concatenate(
            [jnp.concatenate([high, high], axis=1), jnp.concatenate([low, zero], axis=1)], axis=0
        )
        col_two.append(jnp.concatenate([high, low], axis=0))
    x_wide = jnp.concatenate(col_two, axis=1)
    met_in[my_col] = pack((dot_nt(x_wide, x_wide)))

    part_one = [jnp.zeros((count, BLK), F32) for _ in range(n_col)]
    for b in range(n_blk):
        if b == n_blk // 3:
            for peer in others(n_col, my_col):
                push(met_in.at[my_col], met_in.at[my_col], m_r, {"col": peer})
        o = dot_nt(col_lhs[where[1, b]], split[b])
        term = o[:count] + o[count:]
        place = where[0, b]
        for r in range(n_col):
            part_one[r] = part_one[r] + (place == r).astype(F32) * term
    for r in range(n_col):
        p1_out[r] = part_one[r]
    if direct:
        @pl.when(last)
        def _():
            for row in range(FAST):
                push(p1_out.at[0], far_p1.at[my_row], far_r, {"row": row, "col": 0}, far_s)
    for d, peer in enumerate(others(n_col, my_col)):
        push(p1_out.at[peer], p_in.at[d], p_r, {"col": peer})

    own_diag = own[count:count + 1] * x_own
    left = [jnp.concatenate(halves(x_own), axis=0)]
    right = [jnp.concatenate(halves(own_diag), axis=0)]
    near = [upper * half + at for at in range(half)]
    far = [(1 - upper) * half + lax.rem(mirror + at, half) for at in range(1, half)]
    order = near + far + [mirror]
    p_two = [jnp.concatenate(halves(p1_out[at]), axis=0) for at in order]

    def products(left, right):
        return dot_nt(jnp.concatenate(left, axis=1), jnp.concatenate(right, axis=1))

    def spread_out(ats, me):
        for at in ats:
            to = at + (at >= me).astype(jnp.int32)
            push(
                g1_in.at[me], g1_in.at[me], g1_r,
                {"row": lax.rem(to, n_row), "col": to // n_row},
            )

    me = my_col * n_row + my_row
    def gathered(some):
        left, right = [], []
        for at, p_at in some:
            both = jnp.concatenate(halves(row_x[at]), axis=0)
            left += [both, p_at]
            right += [p_at, both]
        return left, right

    pairs = list(zip(order, p_two))
    drain(row_x.at[pl.ds(0, half - 1)], rx_r.at[0])
    one, two = gathered(pairs[:half])
    near_sum = products(left + one, right + two)
    for at, both in zip(near, one[::2]):
        row_lhs[at] = both
    drain(row_x.at[pl.ds(0, half - 1)], rx_r.at[1])
    if direct:
        @pl.when(last)
        def _():
            far_g[...] = pack(near_sum + products(*gathered(pairs[half:-1])))
            for row in range(FAST):
                push(far_g, g1_in.at[me], g1_r, {"row": row, "col": 0})

    drain(row_x.at[pl.ds(0, 1)], rx_r.at[2])
    one, two = gathered(pairs[half:])
    packed = pack(near_sum + products(one, two))
    if direct:
        g1_in[me] = packed

        @pl.when(jnp.logical_not(last))
        def _():
            spread_out(range(FAST), me)

        spread_out(range(FAST, n_row * n_col - 1), me)
    else:
        g1_out[...] = packed
        for d, peer in enumerate(others(n_row, my_row)):
            push(g1_out, g1_in.at[d], g1_r, {"row": peer})

    for at, both in zip(order[half:], one[::2]):
        row_lhs[at] = both

    part_two = [jnp.zeros((count, BLK), F32) for _ in range(n_row)]
    for b in range(n_blk):
        o = dot_nn(row_lhs[where[0, b]], split[b])
        term = o[:count, :BLK] + o[count:, :BLK] + o[:count, BLK:]
        place = where[1, b]
        for q in range(n_row):
            part_two[q] = part_two[q] + (place == q).astype(F32) * term
    for q in range(n_row):
        p2_out[q] = part_two[q]
    for d, peer in enumerate(others(n_row, my_row)):
        push(p2_out.at[peer], p_in.at[n_col - 1 + d], p_r, {"row": peer})

    if not direct:
        drain(g1_in.at[pl.ds(0, n_row - 1)], g1_r)
        g2_out[...] = add([g1_out[...]] + [g1_in[d] for d in range(n_row - 1)])
        for d, peer in enumerate(others(n_col, my_col)):
            push(g2_out, g2_in.at[d], g2_r[0], {"col": peer})

    drain(met_in.at[pl.ds(0, n_col - 1)], m_r)
    metric = unpack(add([met_in[d] for d in range(n_col)]))
    shift = count
    while shift < BLK:
        metric = metric + pltpu.roll(metric, shift, 1)
        shift *= 2
    lines = [jnp.broadcast_to(metric[:, k:k + 1], (count, BLK)) for k in range(count)]
    solved = x_own
    pivots = jnp.ones((count, BLK), F32)
    for k in range(count):
        pivot = lines[k][k:k + 1]
        pivots = jnp.where(sub == k, pivot, pivots)
        ratio = jnp.where(sub == k, 0.0, lines[k] / pivot)
        solved = solved - ratio * solved[k:k + 1]
        for j in range(k + 1, count):
            lines[j] = lines[j] - ratio * lines[j][k:k + 1]
    high, low = halves(solved / pivots)
    y_two = jnp.concatenate(
        [jnp.concatenate([high] * per, axis=0), jnp.concatenate([low] * per, axis=0)], axis=1
    )

    drain(p_in, p_r)
    image = own_diag + p2_out[my_row]
    for d in range(n_row - 1):
        image = image + p_in[n_col - 1 + d]
    image = add([image, p1_out[my_col]] + [p_in[d] for d in range(n_col - 1)])
    out_ref[0] = image

    if direct:
        far_sum[...] = jnp.zeros_like(far_sum)

        @pl.when(first)
        def _():
            col_both = [jnp.concatenate(halves(col_x[row]), axis=0) for row in range(n_row)]
            drain(far_p1, far_r)
            far_left, far_right = [], []
            for row, both in enumerate(col_both):
                p_far = jnp.concatenate(halves(far_p1[row]), axis=0)
                far_left += [both, p_far]
                far_right += [p_far, both]
            far_sum[...] = pack(products(far_left, far_right))

        drain(g1_in.at[pl.ds(0, n_row * n_col - 1)], g1_r)
        gram = add([far_sum[...]] + [g1_in[d] for d in range(n_row * n_col)])
    else:
        drain(g2_in.at[pl.ds(0, n_col - 1)], g2_r[0])
        gram = add([g2_out[...]] + [g2_in[d] for d in range(n_col - 1)])
    wide = unpack(gram)
    o = dot_nn(jnp.concatenate(halves(wide), axis=0), y_two)
    out_ref[1] = image - (o[:count, :BLK] + o[count:, :BLK] + o[:count, BLK:])
    drain(sent, send)
    if direct:
        @pl.when(last)
        def _():
            drain(far_p1.at[pl.ds(0, FAST)], far_s)


def part_kernel(both_ref, image_ref, resid_ref):
    image_ref[...] = both_ref[0]
    resid_ref[...] = both_ref[1]


def per_device(n_row, n_col, vectors, diag_energy, blocks, block_row, block_col):
    count = vectors.shape[0]
    n_blk = blocks.shape[1]
    groups = count // 8
    piece = (count, BLK)
    direct = n_row * n_col <= DIRECT
    n_all = n_row * n_col if direct else n_row
    pieces = 2 * (n_row + n_col - 2)
    small = n_col - 1 + n_all - 1 + (0 if direct else n_col - 1)
    vmem = pl.BlockSpec(memory_space=pltpu.VMEM)
    dma = pltpu.SemaphoreType.DMA
    both = pl.pallas_call(
        functools.partial(kernel, n_row, n_col),
        out_shape=pltpu.VMEM((2,) + piece, F32),
        in_specs=[pl.BlockSpec(memory_space=pl.ANY)] * 5,
        out_specs=vmem,
        scratch_shapes=[
            pltpu.VMEM((count + 8, BLK), F32),
            pltpu.SMEM((2, n_blk), jnp.int32),
            pltpu.VMEM((n_blk, BLK, BLK), F32),
            pltpu.VMEM((n_blk, BLK, 2 * BLK), BF16),
            pltpu.VMEM((n_row,) + piece, F32),
            pltpu.VMEM((n_col,) + piece, F32),
            pltpu.VMEM((n_row, 2 * count, 2 * BLK), BF16),
            pltpu.VMEM((n_col, 2 * count, BLK), BF16),
            pltpu.VMEM((n_col, groups, BLK), F32),
            pltpu.VMEM((n_col,) + piece, F32),
            pltpu.VMEM((n_row,) + piece, F32),
            pltpu.VMEM((n_col + n_row - 2,) + piece, F32),
            pltpu.VMEM((groups, BLK), F32),
            pltpu.VMEM((n_all, groups, BLK), F32),
            pltpu.VMEM((groups, BLK), F32),
            pltpu.VMEM((n_col, groups, BLK), F32),
            pltpu.VMEM((8 * pieces + small, groups, BLK), F32),
            pltpu.VMEM((n_row,) + piece, F32),
            pltpu.VMEM((groups, BLK), F32),
            pltpu.VMEM((groups, BLK), F32),
            dma((3,)),
            dma, dma((3,)), dma, dma, dma, dma,
            *([] if direct else [dma]),
        ],
        compiler_params=pltpu.CompilerParams(collective_id=0, has_side_effects=True),
    )(vectors, diag_energy.reshape(1, -1), block_row, block_col, blocks)
    return pl.pallas_call(
        part_kernel,
        out_shape=[jax.ShapeDtypeStruct(piece, F32)] * 2,
        in_specs=[vmem],
        out_specs=[vmem, vmem],
    )(pltpu.with_memory_space_constraint(both, pltpu.VMEM))


def solution(mesh):
    return jax.shard_map(
        functools.partial(per_device, mesh.shape["row"], mesh.shape["col"]),
        mesh=mesh,
        in_specs=(
            P(None, ("row", "col")),
            P(("row", "col")),
            P("row", "col", None, None),
            P("row", "col"),
            P("row", "col"),
        ),
        out_specs=(P(None, ("row", "col")), P(None, ("row", "col"))),
        check_vma=False,
    )
```

```python
import functools

import jax
import jax.numpy as jnp
from jax import lax
from jax.experimental import pallas as pl
from jax.experimental.pallas import tpu as pltpu
from jax.sharding import PartitionSpec as P

BLK = 128
DIRECT = 64
FAST = 2
F32 = jnp.float32
BF16 = jnp.bfloat16
MESH = pl.DeviceIdType.MESH


def halves(x):
    high = x.astype(BF16)
    return high, (x - high.astype(F32)).astype(BF16)


def add(terms):
    while len(terms) > 1:
        terms = [a + b for a, b in zip(terms[::2], terms[1::2])] + terms[len(terms) & ~1:]
    return terms[0]


def dot_nt(a, b):
    return lax.dot_general(a, b, (((1,), (1,)), ((), ())), preferred_element_type=F32)


def dot_nn(a, b):
    return lax.dot_general(a, b, (((1,), (0,)), ((), ())), preferred_element_type=F32)


def drain(ref, sem):
    pltpu.make_async_copy(ref, ref, sem).wait()


def kernel(
    n_row, n_col,
    x_hbm, diag_hbm, rows_hbm, cols_hbm, blocks_hbm,
    out_ref,
    own, where, tiles, split, col_x, row_x, col_lhs, row_lhs,
    met_in, p1_out, p2_out, p_in, g1_out, g1_in, g2_out, g2_in, sent, far_p1, far_g, far_sum,
    load_sem, cx_r, rx_r, m_r, p_r, g1_r, far_r, *g2_r,
):
    count = x_hbm.shape[0]
    x_ref = own.at[pl.ds(0, count)]
    n_blk = tiles.shape[0]
    my_row = lax.axis_index("row")
    my_col = lax.axis_index("col")
    direct = n_row * n_col <= DIRECT

    send, far_s = load_sem.at[0], load_sem.at[1]
    last = my_col == n_col - 1
    first = (my_col == 0) & (my_row < FAST)

    def push(source, target, recv, peer, sem=send):
        pltpu.make_async_remote_copy(
            src_ref=source, dst_ref=target, send_sem=sem, recv_sem=recv,
            device_id=peer, device_id_type=MESH,
        ).start()

    def others(size, me):
        if size & (size - 1):
            return [lax.rem(me + d, size) for d in range(1, size)]
        return [(me + d) & (size - 1) for d in range(1, size)]

    barrier = pltpu.get_barrier_semaphore()
    for peer in others(n_row, my_row):
        pl.semaphore_signal(barrier, inc=1, device_id={"row": peer}, device_id_type=MESH)
    for peer in others(n_col, my_col):
        pl.semaphore_signal(barrier, inc=1, device_id={"col": peer}, device_id_type=MESH)

    for source, target, at in [
        (x_hbm, x_ref, 0), (diag_hbm, own.at[pl.ds(count, 1)], 0),
        (rows_hbm, where.at[pl.ds(0, 1)], 1), (cols_hbm, where.at[pl.ds(1, 1)], 1), (blocks_hbm.at[0], tiles, 2),
    ]:
        pltpu.make_async_copy(source, target, load_sem.at[at]).start()
    drain(own.at[pl.ds(0, count + 1)], load_sem.at[0])
    mirror = n_col - 1 - my_col
    half = n_col // 2
    upper = (my_col >= half).astype(jnp.int32)
    skip = (my_col == 0).astype(jnp.int32)
    base, step = (n_col - 1) * (1 - upper) - skip, 2 * upper - 1
    across = [base + step * at for at in range(half - 1)] + [base + step * (half - 1) + half * skip]
    beside = [upper * half + ((my_col + at) & (half - 1)) for at in range(1, half)]
    pl.semaphore_wait(barrier, n_row + n_col - 2)

    for peer in across:
        push(x_ref, row_x.at[my_col], rx_r.at[1 + (peer == mirror).astype(jnp.int32)], {"col": peer})
    for peer in beside:
        push(x_ref, row_x.at[my_col], rx_r.at[0], {"col": peer})
    for peer in others(n_row, my_row):
        push(x_ref, col_x.at[my_row], cx_r, {"row": peer})
    x_own = x_ref[...]
    row_x[my_col] = x_own
    col_x[my_row] = x_own

    drain(where, load_sem.at[1])
    drain(tiles, load_sem.at[2])
    for b in range(n_blk):
        high, low = halves(tiles[b])
        split[b] = jnp.concatenate([high, low], axis=1)

    per = BLK // count
    groups = count // 8
    lane = lax.broadcasted_iota(jnp.int32, (count, BLK), 1)
    sub = lax.broadcasted_iota(jnp.int32, (count, BLK), 0)
    keep = (lane // count) == (sub % per)

    def pack(o):
        wide = jnp.concatenate([o[:count], jnp.zeros((count, BLK - 2 * count), F32)], axis=1)
        wide = wide + jnp.concatenate([o[count:, :count], jnp.zeros((count, BLK - count), F32)], axis=1)
        spread = add([wide] + [pltpu.roll(wide, count * at, 1) for at in range(1, per)])
        spread = jnp.where(keep, spread, 0.0)
        return jnp.concatenate(
            [jnp.sum(spread[g * per:(g + 1) * per], axis=0, keepdims=True) for g in range(groups)], axis=0
        )

    def unpack(packed):
        wide = jnp.concatenate(
            [jnp.broadcast_to(packed[g:g + 1], (per, BLK)) for g in range(groups)], axis=0
        )
        return jnp.where(keep, wide, 0.0)

    drain(col_x.at[pl.ds(0, n_row - 1)], cx_r)
    zero = jnp.zeros((count, BLK), BF16)
    col_two = []
    for q in range(n_row):
        high, low = halves(col_x[q])
        col_lhs[q] = jnp.concatenate(
            [jnp.concatenate([high, high], axis=1), jnp.concatenate([low, zero], axis=1)], axis=0
        )
        col_two.append(jnp.concatenate([high, low], axis=0))
    x_wide = jnp.concatenate(col_two, axis=1)
    met_in[my_col] = pack((dot_nt(x_wide, x_wide)))

    part_one = [jnp.zeros((count, BLK), F32) for _ in range(n_col)]
    for b in range(n_blk):
        if b == n_blk // 3:
            for peer in others(n_col, my_col):
                push(met_in.at[my_col], met_in.at[my_col], m_r, {"col": peer})
        o = dot_nt(col_lhs[where[1, b]], split[b])
        term = o[:count] + o[count:]
        place = where[0, b]
        for r in range(n_col):
            part_one[r] = part_one[r] + (place == r).astype(F32) * term
    for r in range(n_col):
        p1_out[r] = part_one[r]
    if direct:
        @pl.when(last)
        def _():
            for row in range(FAST):
                push(p1_out.at[0], far_p1.at[my_row], far_r, {"row": row, "col": 0}, far_s)
    for d, peer in enumerate(others(n_col, my_col)):
        push(p1_out.at[peer], p_in.at[d], p_r, {"col": peer})

    own_diag = own[count:count + 1] * x_own
    left = [jnp.concatenate(halves(x_own), axis=0)]
    right = [jnp.concatenate(halves(own_diag), axis=0)]
    near = [upper * half + at for at in range(half)]
    far = [(1 - upper) * half + lax.rem(mirror + at, half) for at in range(1, half)]
    order = near + far + [mirror]
    p_two = [jnp.concatenate(halves(p1_out[at]), axis=0) for at in order]

    def products(left, right):
        return dot_nt(jnp.concatenate(left, axis=1), jnp.concatenate(right, axis=1))

    def spread_out(ats, me):
        for at in ats:
            to = at + (at >= me).astype(jnp.int32)
            push(
                g1_in.at[me], g1_in.at[me], g1_r,
                {"row": lax.rem(to, n_row), "col": to // n_row},
            )

    me = my_col * n_row + my_row
    def gathered(some):
        left, right = [], []
        for at, p_at in some:
            both = jnp.concatenate(halves(row_x[at]), axis=0)
            left += [both, p_at]
            right += [p_at, both]
        return left, right

    pairs = list(zip(order, p_two))
    drain(row_x.at[pl.ds(0, half - 1)], rx_r.at[0])
    one, two = gathered(pairs[:half])
    near_sum = products(left + one, right + two)
    for at, both in zip(near, one[::2]):
        row_lhs[at] = both
    drain(row_x.at[pl.ds(0, half - 1)], rx_r.at[1])
    if direct:
        @pl.when(last)
        def _():
            far_g[...] = pack(near_sum + products(*gathered(pairs[half:-1])))
            for row in range(FAST):
                push(far_g, g1_in.at[me], g1_r, {"row": row, "col": 0})

    drain(row_x.at[pl.ds(0, 1)], rx_r.at[2])
    one, two = gathered(pairs[half:])
    packed = pack(near_sum + products(one, two))
    if direct:
        g1_in[me] = packed

        @pl.when(jnp.logical_not(last))
        def _():
            spread_out(range(FAST), me)

        spread_out(range(FAST, n_row * n_col - 1), me)
    else:
        g1_out[...] = packed
        for d, peer in enumerate(others(n_row, my_row)):
            push(g1_out, g1_in.at[d], g1_r, {"row": peer})

    for at, both in zip(order[half:], one[::2]):
        row_lhs[at] = both

    part_two = [jnp.zeros((count, BLK), F32) for _ in range(n_row)]
    for b in range(n_blk):
        o = dot_nn(row_lhs[where[0, b]], split[b])
        term = o[:count, :BLK] + o[count:, :BLK] + o[:count, BLK:]
        place = where[1, b]
        for q in range(n_row):
            part_two[q] = part_two[q] + (place == q).astype(F32) * term
    for q in range(n_row):
        p2_out[q] = part_two[q]
    for d, peer in enumerate(others(n_row, my_row)):
        push(p2_out.at[peer], p_in.at[n_col - 1 + d], p_r, {"row": peer})

    if not direct:
        drain(g1_in.at[pl.ds(0, n_row - 1)], g1_r)
        g2_out[...] = add([g1_out[...]] + [g1_in[d] for d in range(n_row - 1)])
        for d, peer in enumerate(others(n_col, my_col)):
            push(g2_out, g2_in.at[d], g2_r[0], {"col": peer})

    drain(met_in.at[pl.ds(0, n_col - 1)], m_r)
    metric = unpack(add([met_in[d] for d in range(n_col)]))
    shift = count
    while shift < BLK:
        metric = metric + pltpu.roll(metric, shift, 1)
        shift *= 2
    lines = [jnp.broadcast_to(metric[:, k:k + 1], (count, BLK)) for k in range(count)]
    solved = x_own
    pivots = jnp.ones((count, BLK), F32)
    for k in range(count):
        pivot = lines[k][k:k + 1]
        pivots = jnp.where(sub == k, pivot, pivots)
        ratio = jnp.where(sub == k, 0.0, lines[k] / pivot)
        solved = solved - ratio * solved[k:k + 1]
        for j in range(k + 1, count):
            lines[j] = lines[j] - ratio * lines[j][k:k + 1]
    high, low = halves(solved / pivots)
    y_two = jnp.concatenate(
        [jnp.concatenate([high] * per, axis=0), jnp.concatenate([low] * per, axis=0)], axis=1
    )

    if direct:
        far_sum[...] = jnp.zeros_like(far_sum)

        @pl.when(first)
        def _():
            col_both = [jnp.concatenate(halves(col_x[row]), axis=0) for row in range(n_row)]
            drain(far_p1, far_r)
            far_left, far_right = [], []
            for row, both in enumerate(col_both):
                p_far = jnp.concatenate(halves(far_p1[row]), axis=0)
                far_left += [both, p_far]
                far_right += [p_far, both]
            far_sum[...] = pack(products(far_left, far_right))

    drain(p_in, p_r)
    image = own_diag + p2_out[my_row]
    for d in range(n_row - 1):
        image = image + p_in[n_col - 1 + d]
    image = add([image, p1_out[my_col]] + [p_in[d] for d in range(n_col - 1)])
    out_ref[0] = image

    if direct:
        drain(g1_in.at[pl.ds(0, n_row * n_col - 1)], g1_r)
        gram = add([far_sum[...]] + [g1_in[d] for d in range(n_row * n_col)])
    else:
        drain(g2_in.at[pl.ds(0, n_col - 1)], g2_r[0])
        gram = add([g2_out[...]] + [g2_in[d] for d in range(n_col - 1)])
    wide = unpack(gram)
    o = dot_nn(jnp.concatenate(halves(wide), axis=0), y_two)
    out_ref[1] = image - (o[:count, :BLK] + o[count:, :BLK] + o[:count, BLK:])
    drain(sent, send)
    if direct:
        @pl.when(last)
        def _():
            drain(far_p1.at[pl.ds(0, FAST)], far_s)


def part_kernel(both_ref, image_ref, resid_ref):
    image_ref[...] = both_ref[0]
    resid_ref[...] = both_ref[1]


def per_device(n_row, n_col, vectors, diag_energy, blocks, block_row, block_col):
    count = vectors.shape[0]
    n_blk = blocks.shape[1]
    groups = count // 8
    piece = (count, BLK)
    direct = n_row * n_col <= DIRECT
    n_all = n_row * n_col if direct else n_row
    pieces = 2 * (n_row + n_col - 2)
    small = n_col - 1 + n_all - 1 + (0 if direct else n_col - 1)
    vmem = pl.BlockSpec(memory_space=pltpu.VMEM)
    dma = pltpu.SemaphoreType.DMA
    both = pl.pallas_call(
        functools.partial(kernel, n_row, n_col),
        out_shape=pltpu.VMEM((2,) + piece, F32),
        in_specs=[pl.BlockSpec(memory_space=pl.ANY)] * 5,
        out_specs=vmem,
        scratch_shapes=[
            pltpu.VMEM((count + 8, BLK), F32),
            pltpu.SMEM((2, n_blk), jnp.int32),
            pltpu.VMEM((n_blk, BLK, BLK), F32),
            pltpu.VMEM((n_blk, BLK, 2 * BLK), BF16),
            pltpu.VMEM((n_row,) + piece, F32),
            pltpu.VMEM((n_col,) + piece, F32),
            pltpu.VMEM((n_row, 2 * count, 2 * BLK), BF16),
            pltpu.VMEM((n_col, 2 * count, BLK), BF16),
            pltpu.VMEM((n_col, groups, BLK), F32),
            pltpu.VMEM((n_col,) + piece, F32),
            pltpu.VMEM((n_row,) + piece, F32),
            pltpu.VMEM((n_col + n_row - 2,) + piece, F32),
            pltpu.VMEM((groups, BLK), F32),
            pltpu.VMEM((n_all, groups, BLK), F32),
            pltpu.VMEM((groups, BLK), F32),
            pltpu.VMEM((n_col, groups, BLK), F32),
            pltpu.VMEM((8 * pieces + small, groups, BLK), F32),
            pltpu.VMEM((n_row,) + piece, F32),
            pltpu.VMEM((groups, BLK), F32),
            pltpu.VMEM((groups, BLK), F32),
            dma((3,)),
            dma, dma((3,)), dma, dma, dma, dma,
            *([] if direct else [dma]),
        ],
        compiler_params=pltpu.CompilerParams(collective_id=0, has_side_effects=True),
    )(vectors, diag_energy.reshape(1, -1), block_row, block_col, blocks)
    return pl.pallas_call(
        part_kernel,
        out_shape=[jax.ShapeDtypeStruct(piece, F32)] * 2,
        in_specs=[vmem],
        out_specs=[vmem, vmem],
    )(pltpu.with_memory_space_constraint(both, pltpu.VMEM))


def solution(mesh):
    return jax.shard_map(
        functools.partial(per_device, mesh.shape["row"], mesh.shape["col"]),
        mesh=mesh,
        in_specs=(
            P(None, ("row", "col")),
            P(("row", "col")),
            P("row", "col", None, None),
            P("row", "col"),
            P("row", "col"),
        ),
        out_specs=(P(None, ("row", "col")), P(None, ("row", "col"))),
        check_vma=False,
    )
```

```python
import functools

import jax
import jax.numpy as jnp
from jax import lax
from jax.experimental import pallas as pl
from jax.experimental.pallas import tpu as pltpu
from jax.sharding import PartitionSpec as P

BLK = 128
DIRECT = 64
FAST = 2
F32 = jnp.float32
BF16 = jnp.bfloat16
MESH = pl.DeviceIdType.MESH


def halves(x):
    high = x.astype(BF16)
    return high, (x - high.astype(F32)).astype(BF16)


def add(terms):
    while len(terms) > 1:
        terms = [a + b for a, b in zip(terms[::2], terms[1::2])] + terms[len(terms) & ~1:]
    return terms[0]


def dot_nt(a, b):
    return lax.dot_general(a, b, (((1,), (1,)), ((), ())), preferred_element_type=F32)


def dot_nn(a, b):
    return lax.dot_general(a, b, (((1,), (0,)), ((), ())), preferred_element_type=F32)


def drain(ref, sem):
    pltpu.make_async_copy(ref, ref, sem).wait()


def kernel(
    n_row, n_col,
    x_hbm, diag_hbm, rows_hbm, cols_hbm, blocks_hbm,
    out_ref,
    own, where, tiles, split, col_x, row_x, col_lhs, row_lhs,
    met_in, p1_out, p2_out, p_in, g1_out, g1_in, g2_out, g2_in, sent, far_p1, far_g, far_sum,
    load_sem, cx_r, rx_r, m_r, p_r, g1_r, far_r, *g2_r,
):
    count = x_hbm.shape[0]
    x_ref = own.at[pl.ds(0, count)]
    n_blk = tiles.shape[0]
    my_row = lax.axis_index("row")
    my_col = lax.axis_index("col")
    direct = n_row * n_col <= DIRECT

    send, far_s = load_sem.at[0], load_sem.at[1]
    last = my_col == n_col - 1
    first = (my_col == 0) & (my_row < FAST)

    def push(source, target, recv, peer, sem=send):
        pltpu.make_async_remote_copy(
            src_ref=source, dst_ref=target, send_sem=sem, recv_sem=recv,
            device_id=peer, device_id_type=MESH,
        ).start()

    def others(size, me):
        if size & (size - 1):
            return [lax.rem(me + d, size) for d in range(1, size)]
        return [(me + d) & (size - 1) for d in range(1, size)]

    barrier = pltpu.get_barrier_semaphore()
    for peer in others(n_row, my_row):
        pl.semaphore_signal(barrier, inc=1, device_id={"row": peer}, device_id_type=MESH)
    for peer in others(n_col, my_col):
        pl.semaphore_signal(barrier, inc=1, device_id={"col": peer}, device_id_type=MESH)

    for source, target, at in [
        (x_hbm, x_ref, 0), (diag_hbm, own.at[pl.ds(count, 1)], 0),
        (rows_hbm, where.at[pl.ds(0, 1)], 1), (cols_hbm, where.at[pl.ds(1, 1)], 1), (blocks_hbm.at[0], tiles, 2),
    ]:
        pltpu.make_async_copy(source, target, load_sem.at[at]).start()
    drain(own.at[pl.ds(0, count + 1)], load_sem.at[0])
    mirror = n_col - 1 - my_col
    half = n_col // 2
    upper = (my_col >= half).astype(jnp.int32)
    skip = (my_col == 0).astype(jnp.int32)
    base, step = (n_col - 1) * (1 - upper) - skip, 2 * upper - 1
    across = [base + step * at for at in range(half - 1)] + [base + step * (half - 1) + half * skip]
    beside = [upper * half + ((my_col + at) & (half - 1)) for at in range(1, half)]
    pl.semaphore_wait(barrier, n_row + n_col - 2)

    for peer in others(n_row, my_row):
        push(x_ref, col_x.at[my_row], cx_r, {"row": peer})
    for peer in across:
        push(x_ref, row_x.at[my_col], rx_r.at[1 + (peer == mirror).astype(jnp.int32)], {"col": peer})
    for peer in beside:
        push(x_ref, row_x.at[my_col], rx_r.at[0], {"col": peer})
    x_own = x_ref[...]
    row_x[my_col] = x_own
    col_x[my_row] = x_own

    drain(where, load_sem.at[1])
    drain(tiles, load_sem.at[2])
    for b in range(n_blk):
        high, low = halves(tiles[b])
        split[b] = jnp.concatenate([high, low], axis=1)

    per = BLK // count
    groups = count // 8
    lane = lax.broadcasted_iota(jnp.int32, (count, BLK), 1)
    sub = lax.broadcasted_iota(jnp.int32, (count, BLK), 0)
    keep = (lane // count) == (sub % per)

    def pack(o):
        wide = jnp.concatenate([o[:count], jnp.zeros((count, BLK - 2 * count), F32)], axis=1)
        wide = wide + jnp.concatenate([o[count:, :count], jnp.zeros((count, BLK - count), F32)], axis=1)
        spread = add([wide] + [pltpu.roll(wide, count * at, 1) for at in range(1, per)])
        spread = jnp.where(keep, spread, 0.0)
        return jnp.concatenate(
            [jnp.sum(spread[g * per:(g + 1) * per], axis=0, keepdims=True) for g in range(groups)], axis=0
        )

    def unpack(packed):
        wide = jnp.concatenate(
            [jnp.broadcast_to(packed[g:g + 1], (per, BLK)) for g in range(groups)], axis=0
        )
        return jnp.where(keep, wide, 0.0)

    drain(col_x.at[pl.ds(0, n_row - 1)], cx_r)
    zero = jnp.zeros((count, BLK), BF16)
    col_two = []
    for q in range(n_row):
        high, low = halves(col_x[q])
        col_lhs[q] = jnp.concatenate(
            [jnp.concatenate([high, high], axis=1), jnp.concatenate([low, zero], axis=1)], axis=0
        )
        col_two.append(jnp.concatenate([high, low], axis=0))
    x_wide = jnp.concatenate(col_two, axis=1)
    met_in[my_col] = pack((dot_nt(x_wide, x_wide)))

    part_one = [jnp.zeros((count, BLK), F32) for _ in range(n_col)]
    for b in range(n_blk):
        if b == n_blk // 3:
            for peer in others(n_col, my_col):
                push(met_in.at[my_col], met_in.at[my_col], m_r, {"col": peer})
        o = dot_nt(col_lhs[where[1, b]], split[b])
        term = o[:count] + o[count:]
        place = where[0, b]
        for r in range(n_col):
            part_one[r] = part_one[r] + (place == r).astype(F32) * term
    for r in range(n_col):
        p1_out[r] = part_one[r]
    if direct:
        @pl.when(last)
        def _():
            for row in range(FAST):
                push(p1_out.at[0], far_p1.at[my_row], far_r, {"row": row, "col": 0}, far_s)
    for d, peer in enumerate(others(n_col, my_col)):
        push(p1_out.at[peer], p_in.at[d], p_r, {"col": peer})

    own_diag = own[count:count + 1] * x_own
    left = [jnp.concatenate(halves(x_own), axis=0)]
    right = [jnp.concatenate(halves(own_diag), axis=0)]
    near = [upper * half + at for at in range(half)]
    far = [(1 - upper) * half + lax.rem(mirror + at, half) for at in range(1, half)]
    order = near + far + [mirror]
    p_two = [jnp.concatenate(halves(p1_out[at]), axis=0) for at in order]

    def products(left, right):
        return dot_nt(jnp.concatenate(left, axis=1), jnp.concatenate(right, axis=1))

    def spread_out(ats, me):
        for at in ats:
            to = at + (at >= me).astype(jnp.int32)
            push(
                g1_in.at[me], g1_in.at[me], g1_r,
                {"row": lax.rem(to, n_row), "col": to // n_row},
            )

    me = my_col * n_row + my_row
    def gathered(some):
        left, right = [], []
        for at, p_at in some:
            both = jnp.concatenate(halves(row_x[at]), axis=0)
            left += [both, p_at]
            right += [p_at, both]
        return left, right

    pairs = list(zip(order, p_two))
    drain(row_x.at[pl.ds(0, half - 1)], rx_r.at[0])
    one, two = gathered(pairs[:half])
    near_sum = products(left + one, right + two)
    for at, both in zip(near, one[::2]):
        row_lhs[at] = both
    drain(row_x.at[pl.ds(0, half - 1)], rx_r.at[1])
    if direct:
        @pl.when(last)
        def _():
            far_g[...] = pack(near_sum + products(*gathered(pairs[half:-1])))
            for row in range(FAST):
                push(far_g, g1_in.at[me], g1_r, {"row": row, "col": 0})

    drain(row_x.at[pl.ds(0, 1)], rx_r.at[2])
    one, two = gathered(pairs[half:])
    packed = pack(near_sum + products(one, two))
    if direct:
        g1_in[me] = packed

        @pl.when(jnp.logical_not(last))
        def _():
            spread_out(range(FAST), me)

        spread_out(range(FAST, n_row * n_col - 1), me)
    else:
        g1_out[...] = packed
        for d, peer in enumerate(others(n_row, my_row)):
            push(g1_out, g1_in.at[d], g1_r, {"row": peer})

    for at, both in zip(order[half:], one[::2]):
        row_lhs[at] = both

    part_two = [jnp.zeros((count, BLK), F32) for _ in range(n_row)]
    for b in range(n_blk):
        o = dot_nn(row_lhs[where[0, b]], split[b])
        term = o[:count, :BLK] + o[count:, :BLK] + o[:count, BLK:]
        place = where[1, b]
        for q in range(n_row):
            part_two[q] = part_two[q] + (place == q).astype(F32) * term
    for q in range(n_row):
        p2_out[q] = part_two[q]
    for d, peer in enumerate(others(n_row, my_row)):
        push(p2_out.at[peer], p_in.at[n_col - 1 + d], p_r, {"row": peer})

    if not direct:
        drain(g1_in.at[pl.ds(0, n_row - 1)], g1_r)
        g2_out[...] = add([g1_out[...]] + [g1_in[d] for d in range(n_row - 1)])
        for d, peer in enumerate(others(n_col, my_col)):
            push(g2_out, g2_in.at[d], g2_r[0], {"col": peer})

    drain(met_in.at[pl.ds(0, n_col - 1)], m_r)
    metric = unpack(add([met_in[d] for d in range(n_col)]))
    shift = count
    while shift < BLK:
        metric = metric + pltpu.roll(metric, shift, 1)
        shift *= 2
    lines = [jnp.broadcast_to(metric[:, k:k + 1], (count, BLK)) for k in range(count)]
    solved = x_own
    pivots = jnp.ones((count, BLK), F32)
    for k in range(count):
        pivot = lines[k][k:k + 1]
        pivots = jnp.where(sub == k, pivot, pivots)
        ratio = jnp.where(sub == k, 0.0, lines[k] / pivot)
        solved = solved - ratio * solved[k:k + 1]
        for j in range(k + 1, count):
            lines[j] = lines[j] - ratio * lines[j][k:k + 1]
    high, low = halves(solved / pivots)
    y_two = jnp.concatenate(
        [jnp.concatenate([high] * per, axis=0), jnp.concatenate([low] * per, axis=0)], axis=1
    )

    if direct:
        far_sum[...] = jnp.zeros_like(far_sum)

        @pl.when(first)
        def _():
            col_both = [jnp.concatenate(halves(col_x[row]), axis=0) for row in range(n_row)]
            drain(far_p1, far_r)
            far_left, far_right = [], []
            for row, both in enumerate(col_both):
                p_far = jnp.concatenate(halves(far_p1[row]), axis=0)
                far_left += [both, p_far]
                far_right += [p_far, both]
            far_sum[...] = pack(products(far_left, far_right))

    drain(p_in, p_r)
    image = own_diag + p2_out[my_row]
    for d in range(n_row - 1):
        image = image + p_in[n_col - 1 + d]
    image = add([image, p1_out[my_col]] + [p_in[d] for d in range(n_col - 1)])
    out_ref[0] = image

    if direct:
        drain(g1_in.at[pl.ds(0, n_row * n_col - 1)], g1_r)
        gram = add([far_sum[...]] + [g1_in[d] for d in range(n_row * n_col)])
    else:
        drain(g2_in.at[pl.ds(0, n_col - 1)], g2_r[0])
        gram = add([g2_out[...]] + [g2_in[d] for d in range(n_col - 1)])
    wide = unpack(gram)
    o = dot_nn(jnp.concatenate(halves(wide), axis=0), y_two)
    out_ref[1] = image - (o[:count, :BLK] + o[count:, :BLK] + o[:count, BLK:])
    drain(sent, send)
    if direct:
        @pl.when(last)
        def _():
            drain(far_p1.at[pl.ds(0, FAST)], far_s)


def part_kernel(both_ref, image_ref, resid_ref):
    image_ref[...] = both_ref[0]
    resid_ref[...] = both_ref[1]


def per_device(n_row, n_col, vectors, diag_energy, blocks, block_row, block_col):
    count = vectors.shape[0]
    n_blk = blocks.shape[1]
    groups = count // 8
    piece = (count, BLK)
    direct = n_row * n_col <= DIRECT
    n_all = n_row * n_col if direct else n_row
    pieces = 2 * (n_row + n_col - 2)
    small = n_col - 1 + n_all - 1 + (0 if direct else n_col - 1)
    vmem = pl.BlockSpec(memory_space=pltpu.VMEM)
    dma = pltpu.SemaphoreType.DMA
    both = pl.pallas_call(
        functools.partial(kernel, n_row, n_col),
        out_shape=pltpu.VMEM((2,) + piece, F32),
        in_specs=[pl.BlockSpec(memory_space=pl.ANY)] * 5,
        out_specs=vmem,
        scratch_shapes=[
            pltpu.VMEM((count + 8, BLK), F32),
            pltpu.SMEM((2, n_blk), jnp.int32),
            pltpu.VMEM((n_blk, BLK, BLK), F32),
            pltpu.VMEM((n_blk, BLK, 2 * BLK), BF16),
            pltpu.VMEM((n_row,) + piece, F32),
            pltpu.VMEM((n_col,) + piece, F32),
            pltpu.VMEM((n_row, 2 * count, 2 * BLK), BF16),
            pltpu.VMEM((n_col, 2 * count, BLK), BF16),
            pltpu.VMEM((n_col, groups, BLK), F32),
            pltpu.VMEM((n_col,) + piece, F32),
            pltpu.VMEM((n_row,) + piece, F32),
            pltpu.VMEM((n_col + n_row - 2,) + piece, F32),
            pltpu.VMEM((groups, BLK), F32),
            pltpu.VMEM((n_all, groups, BLK), F32),
            pltpu.VMEM((groups, BLK), F32),
            pltpu.VMEM((n_col, groups, BLK), F32),
            pltpu.VMEM((8 * pieces + small, groups, BLK), F32),
            pltpu.VMEM((n_row,) + piece, F32),
            pltpu.VMEM((groups, BLK), F32),
            pltpu.VMEM((groups, BLK), F32),
            dma((3,)),
            dma, dma((3,)), dma, dma, dma, dma,
            *([] if direct else [dma]),
        ],
        compiler_params=pltpu.CompilerParams(collective_id=0, has_side_effects=True),
    )(vectors, diag_energy.reshape(1, -1), block_row, block_col, blocks)
    return pl.pallas_call(
        part_kernel,
        out_shape=[jax.ShapeDtypeStruct(piece, F32)] * 2,
        in_specs=[vmem],
        out_specs=[vmem, vmem],
    )(pltpu.with_memory_space_constraint(both, pltpu.VMEM))


def solution(mesh):
    return jax.shard_map(
        functools.partial(per_device, mesh.shape["row"], mesh.shape["col"]),
        mesh=mesh,
        in_specs=(
            P(None, ("row", "col")),
            P(("row", "col")),
            P("row", "col", None, None),
            P("row", "col"),
            P("row", "col"),
        ),
        out_specs=(P(None, ("row", "col")), P(None, ("row", "col"))),
        check_vma=False,
    )
```
